32 devices in a mesh: seq: 8 (over z, x), fsdp: 4 (over y, core).
Axes of the slice: x: 2, y: 2, z: 4, core: 2. Of those that a mesh axis runs over, the one named last changes fastest.
Arguments:
- tokens: bfloat16 [4, 1024, 1024], P('fsdp', 'seq'), may hold values from -6 to 6
- cotangent: bfloat16 [4, 1024, 1024], P('fsdp', 'seq'), may hold values from -6 to 6
- segments: int32 [4, 1024], P('fsdp', 'seq'), may hold values from 0 to 7, never falling along the last dimension, each value on 1 to 512 neighbouring positions
- weight_in: float32 [6144, 1024], P('fsdp'), may hold values from -0.1875 to 0.1875
- weight_out: float32 [2048, 1024], P('fsdp'), may hold values from -0.1875 to 0.1875
- weight_up: float32 [5632, 1024], P('fsdp'), may hold values from -0.1875 to 0.1875
- weight_down: float32 [2816, 1024], P('fsdp'), may hold values from -0.21875 to 0.21875
- vectors: float32 [35088], replicated, may hold values from -14 to 3, as said below
- momentum_in: float32 [6144, 1024], P(('seq', 'fsdp')), may hold values from -9.1552734e-05 to 9.1552734e-05
- momentum_out: float32 [2048, 1024], P(('seq', 'fsdp')), may hold values from -9.1552734e-05 to 9.1552734e-05
- momentum_up: float32 [5632, 1024], P(('seq', 'fsdp')), may hold values from -9.1552734e-05 to 9.1552734e-05
- momentum_down: float32 [2816, 1024], P(('seq', 'fsdp')), may hold values from -9.1552734e-05 to 9.1552734e-05
- first_moment: float32 [35088], replicated, may hold values from -0.00018310547 to 0.00018310547
- second_moment: float32 [35088], replicated, may hold values from 1e-09 to 1e-08
Outputs:
- mixed: bfloat16 [4, 1024, 1024], P('fsdp', 'seq')
- grad_tokens: float32 [4, 1024, 1024], P('fsdp', 'seq')
- grad_in: float32 [6144, 1024], P(('seq', 'fsdp'))
- grad_out: float32 [2048, 1024], P(('seq', 'fsdp'))
- grad_up: float32 [5632, 1024], P(('seq', 'fsdp'))
- grad_down: float32 [2816, 1024], P(('seq', 'fsdp'))
- renewed_in: float32 [6144, 1024], P(('seq', 'fsdp'))
- renewed_out: float32 [2048, 1024], P(('seq', 'fsdp'))
- renewed_up: float32 [5632, 1024], P(('seq', 'fsdp'))
- renewed_down: float32 [2816, 1024], P(('seq', 'fsdp'))
- update_in: float32 [6144, 1024], P(('seq', 'fsdp'))
- update_out: float32 [2048, 1024], P(('seq', 'fsdp'))
- update_up: float32 [5632, 1024], P(('seq', 'fsdp'))
- update_down: float32 [2816, 1024], P(('seq', 'fsdp'))
- grad_vector: float32 [35088], replicated
- first_next: float32 [35088], replicated
- second_next: float32 [35088], replicated
- update_vector: float32 [35088], replicated
- grad_norm: float32 [1], replicated
The draws below stay inside these ranges and needn't reach their ends.
Inputs may be any that keep to these rules, and one draw needn't show every extreme that they name: `segments`: within a row the document numbers never fall; every document of 0 .. 7 has 1 to 512 tokens, and one has exactly 512. `vectors`: gains lie between 0.5 and 1.5, exp(decay_log) between 1 and 16.
All inputs are finite; a program needn't handle non-finite values.
Results may differ from the reference program's by a relative error of at most 0.01.
The reference program's roundings to bfloat16 on the way count: a program that leaves them out, or rounds other values in their place, can miss the bound.
Values may be sent and summed in bfloat16 or wider, within the bound.
No kernel may reach another device: no remote copies, remote signals or barrier semaphores. Data moves between devices by JAX's collectives and lax.ppermute only.
A program may use at most 320 MiB of HBM per device.

```python
import math
from functools import partial
import jax
import jax.numpy as jnp
import numpy as np
from jax import lax

D = 1024
H = 8
DKH = 128
DVH = 256
FF = 2816
KCONV = 4
STRETCH = 64
NS_ITERS = 2
STEP = 10
DV = 2048
CONV_CH = 4096
IN_ROWS = 6144
NVEC = 35088
LEN = 1024
SEQS = 4
DOCS = 8
MOST = 512


def draw_vectors(key, part):
    pieces_key = jax.random.split(key, 5)
    conv_width = 2 * H * DKH + H * DVH
    small_weights = jax.random.normal(pieces_key[0], (2 * H * D,), jnp.float32) * D ** (-0.5)
    rate_floor = math.log(1e-05)
    rate_ceiling = math.log(0.05)
    tap_weights = jax.random.uniform(pieces_key[1], (KCONV * conv_width,), jnp.float32, -1.0, 1.0)
    gains = 1.0 + 0.5 * jax.random.uniform(pieces_key[2], (2 * D + DVH,), jnp.float32, -1.0, 1.0)
    decay_log = jnp.log(jax.random.uniform(pieces_key[3], (H,), jnp.float32, 1.0, 16.0))
    step_size = jnp.exp(jax.random.uniform(pieces_key[4], (H,), jnp.float32, rate_floor, rate_ceiling))
    decay_bias = step_size + jnp.log(-jnp.expm1(-step_size))
    return jnp.concatenate([small_weights, tap_weights, gains, decay_log, decay_bias])


def block_scale(key, shape, cuts, low, top_value):
    loudness = 1.0
    for position, shards_of in cuts:
        steps = jax.random.uniform(jax.random.fold_in(jax.random.fold_in(key, 6), position), (shards_of,), jnp.float32, low / len(cuts), top_value / len(cuts))
        loudness = loudness * jnp.repeat(jnp.exp(steps), shape[position] // shards_of).reshape((-1,) + (1,) * (len(shape) - 1 - position))
    return loudness


def profile(count, total, most, skew):
    loads = [(1 << 20) // math.isqrt(rank ** skew) + 1 for rank in range(2, count + 1)]
    spare, given = total - most - (count - 1), [1] * (count - 1)
    while spare > 0:
        free = [i for i in range(count - 1) if given[i] < most]
        pool, left = sum([loads[i] for i in free]), spare
        for i in free:
            more = min(most - given[i], max(1, left * loads[i] // pool), spare)
            given[i] = given[i] + more
            spare = spare - more
    return np.array([most] + given)


def uneven(stream_key, amount, total, reach, slope):
    if amount == 2:
        one = jax.random.randint(stream_key, (), max(1, total - reach), min(reach, total - 1) + 1)
        return jnp.stack([one, total - one])
    tallies = jnp.asarray(profile(amount, total, reach, slope), jnp.int32)
    pairs = (amount - 1) // 2
    donor, sink = tallies[1:1 + 2 * pairs:2], tallies[2:2 + 2 * pairs:2]
    room = jnp.minimum(donor - 1, reach - sink)
    moved = jax.random.randint(jax.random.fold_in(stream_key, 1), (pairs,), 0, 1 << 20) % (room + 1)
    tallies = tallies.at[1:1 + 2 * pairs:2].set(donor - moved).at[2:2 + 2 * pairs:2].set(sink + moved)
    return tallies[jax.random.permutation(jax.random.fold_in(stream_key, 2), amount)]


def normal_values(own_key, extent, scale, bound, cuts=(), held_as=jnp.bfloat16):
    level = block_scale(own_key, extent, cuts, -0.22, 0.18) if cuts else 1.0
    entries = jax.random.normal(own_key, extent, jnp.float32) * scale * level
    return jnp.minimum(jnp.maximum(entries, -bound), bound).astype(held_as)


def setup_inputs(seed: int = 0) -> dict:
    splits = jax.random.split(jax.random.key(seed), 15)
    tokens = normal_values(splits[0], (SEQS, LEN, D), 1.0, 6.0, ((0, 4), (1, 8)))
    cotangent = normal_values(splits[1], (SEQS, LEN, D), 1.0, 6.0, ((0, 4), (1, 8)))
    segments = jax.vmap(lambda own: jnp.searchsorted(jnp.cumsum(uneven(own, DOCS, LEN, MOST, 2)), jnp.arange(LEN), side="right"))(jax.random.split(splits[2], SEQS)).reshape((SEQS, LEN)).astype(jnp.int32)
    weight_in = normal_values(splits[3], (IN_ROWS, D), D ** -0.5, 0.1875, ((0, 4),), jnp.float32)
    weight_out = normal_values(splits[4], (DV, D), (DV // 2) ** -0.5, 0.1875, ((0, 4),), jnp.float32)
    weight_up = normal_values(splits[5], (2 * FF, D), D ** -0.5, 0.1875, ((0, 4),), jnp.float32)
    weight_down = normal_values(splits[6], (FF, D), (FF // 4) ** -0.5, 0.21875, ((0, 4),), jnp.float32)
    vectors = draw_vectors(jax.random.fold_in(splits[14], 71), 0)
    momentum_in = normal_values(splits[8], (IN_ROWS, D), (1.5e-5), 9.1552734375e-05, ((0, 32),), jnp.float32)
    momentum_out = normal_values(splits[9], (DV, D), (1.5e-5), 9.1552734375e-05, ((0, 32),), jnp.float32)
    momentum_up = normal_values(splits[10], (2 * FF, D), (1.5e-5), 9.1552734375e-05, ((0, 32),), jnp.float32)
    momentum_down = normal_values(splits[11], (FF, D), (1.5e-5), 9.1552734375e-05, ((0, 32),), jnp.float32)
    first_moment = normal_values(splits[12], (NVEC,), (3e-5), 0.00018310547, (), jnp.float32)
    second_moment = jnp.clip(jnp.exp(jax.random.uniform(splits[13], (NVEC,), jnp.float32, math.log(9.999999717180685e-10), math.log(9.99999993922529e-09))), 9.999999717180685e-10, 9.99999993922529e-09)
    return {"tokens": tokens, "cotangent": cotangent, "segments": segments, "weight_in": weight_in, "weight_out": weight_out, "weight_up": weight_up, "weight_down": weight_down, "vectors": vectors, "momentum_in": momentum_in, "momentum_out": momentum_out, "momentum_up": momentum_up, "momentum_down": momentum_down, "first_moment": first_moment, "second_moment": second_moment}


PRECISE = lax.Precision.HIGHEST
RMS_EPS = 1e-06
NS_A = 3.4445
NS_B = -4.775
NS_C = 2.0315
MOMENTUM = 0.95
ADAM_ONE = 0.9
ADAM_TWO = 0.95
LEARN_RATE = 0.02
VECTOR_RATE = 0.01
CLIP_NORM = 1.0
ADAM_EPS = 1e-08

@jax.custom_vjp
def low(v):
    return lax.optimization_barrier(v.astype(jnp.bfloat16)).astype(jnp.float32)

@jax.custom_vjp
def low_back(v):
    return v

def low_keep(v):
    return (low(v), None)

def low_pass(kept, grad):
    return (grad,)

def back_keep(v):
    return (v, None)

def back_low(kept, grad):
    return (low(grad),)
low.defvjp(low_keep, low_pass)
low_back.defvjp(back_keep, back_low)

def unpack_vectors(vectors):
    widths = [2 * H * D, KCONV * (2 * H * DKH + H * DVH), D, D, DVH, H, H]
    pieces = []
    offset = 0
    for span_width in widths:
        pieces.append(vectors[offset:offset + span_width])
        offset += span_width
    projection = pieces[0].reshape(2 * H, D)
    conv_taps = pieces[1].reshape(KCONV, 2 * H * DKH + H * DVH)
    return (projection, conv_taps, pieces[2], pieces[3], pieces[4], pieces[5], pieces[6])

def rms_scale(values, gain):
    inverse = lax.rsqrt(lax.optimization_barrier(jnp.mean(values * values, axis=-1, keepdims=True)) + RMS_EPS)
    return values * inverse * gain

def swiglu(values):
    return jax.nn.silu(values[:, :FF]) * values[:, FF:]

def short_conv(extended, extended_ids, tap_weights):
    out_rows = extended.shape[0] - (KCONV - 1)
    current_ids = extended_ids[KCONV - 1:]
    summed = jnp.zeros((out_rows, extended.shape[1]), jnp.float32)
    for tap_index in range(KCONV):
        same_document = (extended_ids[tap_index:tap_index + out_rows] == current_ids).astype(jnp.float32)
        summed = summed + tap_weights[tap_index] * extended[tap_index:tap_index + out_rows] * same_document[:, None]
    return jax.nn.silu(summed)

def delta_block(carry_state, block_inputs):
    queries, keys_unit, values, beta_rates, log_decay, block_ids, before_id = block_inputs
    length_block = block_ids.shape[0]
    cumulative = jnp.cumsum(log_decay, axis=0).T
    row_index = lax.broadcasted_iota(jnp.int32, (length_block, length_block), 0)
    col_index = lax.broadcasted_iota(jnp.int32, (length_block, length_block), 1)
    linked = (row_index >= col_index) & (block_ids[:, None] == block_ids[None, :])
    spread = cumulative[:, :, None] - cumulative[:, None, :]
    ratios = jnp.where(linked[None], jnp.exp(jnp.where(linked[None], spread, 0.0)), 0.0)
    carried = jnp.exp(cumulative) * (block_ids == before_id).astype(jnp.float32)[None, :]
    beta_heads = beta_rates.T
    key_gram = jnp.einsum('thd,shd->hts', keys_unit, keys_unit, precision=PRECISE)
    cross_gram = jnp.einsum('thd,shd->hts', queries, keys_unit, precision=PRECISE)
    strict = jnp.where((row_index > col_index)[None], ratios * key_gram, 0.0)
    system = jnp.eye(length_block, dtype=jnp.float32)[None] + beta_heads[:, :, None] * strict
    key_state = jnp.einsum('thd,hdw->htw', keys_unit, carry_state, precision=PRECISE)
    value_heads = jnp.transpose(values, (1, 0, 2))
    target = beta_heads[:, :, None] * (value_heads - carried[:, :, None] * key_state)
    solved = jax.scipy.linalg.solve_triangular(system, target, lower=True, unit_diagonal=True)
    query_state = jnp.einsum('thd,hdw->htw', queries, carry_state, precision=PRECISE)
    outputs = carried[:, :, None] * query_state + jnp.einsum('hts,hsw->htw', ratios * cross_gram, solved, precision=PRECISE)
    last_ratios = ratios[:, length_block - 1, :]
    new_state = carried[:, length_block - 1][:, None, None] * carry_state + jnp.einsum('shd,hs,hsw->hdw', keys_unit, last_ratios, solved, precision=PRECISE)
    return (new_state, jnp.transpose(outputs, (1, 0, 2)))

def mixer_core(extended, extended_ids, normed_in, tap_weights, small_weights, decay_log, decay_bias, start_state, first_id):
    count_rows = normed_in.shape[0]
    conv_out = short_conv(extended, extended_ids, tap_weights)
    small = jnp.dot(normed_in, small_weights.T, precision=PRECISE)
    beta_rates = jax.nn.sigmoid(small[:, :H])
    log_decay = -jnp.exp(decay_log) * jax.nn.softplus(small[:, H:] + decay_bias)
    queries = conv_out[:, :H * DKH].reshape(count_rows, H, DKH)
    queries = queries * lax.rsqrt(lax.optimization_barrier(jnp.sum(queries * queries, axis=-1, keepdims=True)) + RMS_EPS) * DKH ** (-0.5)
    keys_unit = conv_out[:, H * DKH:2 * H * DKH].reshape(count_rows, H, DKH)
    keys_unit = keys_unit * lax.rsqrt(lax.optimization_barrier(jnp.sum(keys_unit * keys_unit, axis=-1, keepdims=True)) + RMS_EPS)
    values = conv_out[:, 2 * H * DKH:].reshape(count_rows, H, DVH)
    extra_width = start_state.shape[2] - DVH
    values = jnp.concatenate([values, jnp.zeros((count_rows, H, extra_width), jnp.float32)], axis=2)
    blocks = count_rows // STRETCH
    row_ids = extended_ids[KCONV - 1:].reshape(blocks, STRETCH)
    before_ids = jnp.concatenate([jnp.reshape(first_id, (1,)), row_ids[:blocks - 1, STRETCH - 1]])
    final_state, outputs = lax.scan(jax.checkpoint(delta_block), start_state, (queries.reshape(blocks, STRETCH, H, DKH), keys_unit.reshape(blocks, STRETCH, H, DKH), values.reshape(blocks, STRETCH, H, start_state.shape[2]), beta_rates.reshape(blocks, STRETCH, H), log_decay.reshape(blocks, STRETCH, H), row_ids, before_ids))
    return (outputs.reshape(count_rows, H, start_state.shape[2]), final_state)

def muon_update(block_rows, gram, total_rows):
    inverse_norm = 1.0 / (jnp.sqrt(jnp.trace(gram)) + 1e-07)
    current = gram * (inverse_norm * inverse_norm)
    identity = jnp.eye(gram.shape[0], dtype=jnp.float32)
    ortho = block_rows * inverse_norm
    for iteration in range(NS_ITERS):
        square = jnp.dot(current, current, precision=PRECISE)
        factor = NS_A * identity + NS_B * current + NS_C * square
        ortho = jnp.dot(ortho, factor, precision=PRECISE)
        if iteration + 1 < NS_ITERS:
            current = jnp.dot(current, jnp.dot(factor, factor, precision=PRECISE), precision=PRECISE)
    return -LEARN_RATE * 0.2 * math.sqrt(max(total_rows, D)) * ortho

def forward_pass(token_values, weight_in, weight_out, weight_up, weight_down, vectors, id_plus):
    projection, conv_taps, gain_one, gain_two, gain_head, decay_log, decay_bias = unpack_vectors(vectors)
    lowered_in = low(weight_in)
    lowered_out = low(weight_out)
    lowered_up = low(weight_up)
    lowered_down = low(weight_down)

    def one_sequence(paired):
        token_rows, row_ids = paired
        normed = low(rms_scale(token_rows, gain_one))
        projected = low(low_back(jnp.dot(normed, lowered_in.T, precision=PRECISE)))
        conv_in = projected[:, :CONV_CH]
        gate_in = projected[:, CONV_CH:]
        extended = jnp.concatenate([jnp.zeros((KCONV - 1, CONV_CH), jnp.float32), conv_in], axis=0)
        extended_ids = jnp.concatenate([jnp.zeros((KCONV - 1,), jnp.float32), row_ids])
        start_state = jnp.zeros((H, DKH, DVH), jnp.float32)
        recurrent, final_state = mixer_core(extended, extended_ids, normed, conv_taps, projection, decay_log, decay_bias, start_state, jnp.zeros((), jnp.float32))
        gated = low(rms_scale(recurrent, gain_head).reshape(LEN, DV) * jax.nn.silu(gate_in))
        attention = low_back(jnp.dot(gated, lowered_out, precision=PRECISE))
        residual = token_rows + attention
        normed_two = low(rms_scale(residual, gain_two))
        gate_up = low_back(jnp.dot(normed_two, lowered_up.T, precision=PRECISE))
        hidden = low(swiglu(gate_up))
        return residual + low_back(jnp.dot(hidden, lowered_down, precision=PRECISE))
    return lax.map(one_sequence, (token_values, id_plus))

def reference(tokens, cotangent, segments, weight_in, weight_out, weight_up, weight_down, vectors, momentum_in, momentum_out, momentum_up, momentum_down, first_moment, second_moment):
    id_plus = segments.astype(jnp.float32) + 1.0
    mixed, pullback = jax.vjp(partial(forward_pass, id_plus=id_plus), tokens.astype(jnp.float32), weight_in, weight_out, weight_up, weight_down, vectors)
    grad_tokens, grad_in, grad_out, grad_up, grad_down, grad_vector = pullback(cotangent.astype(jnp.float32))
    squares = jnp.sum(grad_in * grad_in) + jnp.sum(grad_out * grad_out) + jnp.sum(grad_up * grad_up) + jnp.sum(grad_down * grad_down) + jnp.sum(grad_vector * grad_vector)
    grad_norm = jnp.sqrt(squares)
    clipping = jnp.minimum(1.0, CLIP_NORM / (grad_norm + 1e-06))
    renewed_list = []
    update_list = []
    for grad_full, momentum in ((grad_in, momentum_in), (grad_out, momentum_out), (grad_up, momentum_up), (grad_down, momentum_down)):
        renewed = MOMENTUM * momentum + (1.0 - MOMENTUM) * clipping * grad_full
        gram = jnp.dot(renewed.T, renewed, precision=PRECISE)
        renewed_list.append(renewed)
        update_list.append(muon_update(renewed, gram, renewed.shape[0]))
    clipped = clipping * grad_vector
    first_next = ADAM_ONE * first_moment + (1.0 - ADAM_ONE) * clipped
    second_next = ADAM_TWO * second_moment + (1.0 - ADAM_TWO) * clipped * clipped
    update_vector = -VECTOR_RATE * (first_next / (1.0 - ADAM_ONE ** STEP)) / (jnp.sqrt(second_next / (1.0 - ADAM_TWO ** STEP)) + ADAM_EPS)
    return (mixed.astype(jnp.bfloat16), grad_tokens, grad_in, grad_out, grad_up, grad_down, renewed_list[0], renewed_list[1], renewed_list[2], renewed_list[3], update_list[0], update_list[1], update_list[2], update_list[3], grad_vector, first_next, second_next, update_vector, grad_norm.reshape(1))
```

```python
import math

import jax
import jax.numpy as jnp
from jax import lax
from jax.sharding import PartitionSpec as P

D = 1024
H = 8
DKH = 128
DVH = 256
FF = 2816
KCONV = 4
STRETCH = 64
NS_ITERS = 2
STEP = 10


PRECISE = lax.Precision.HIGHEST
RMS_EPS = 1e-06
NS_A = 3.4445
NS_B = -4.775
NS_C = 2.0315
MOMENTUM = 0.95
ADAM_ONE = 0.9
ADAM_TWO = 0.95
LEARN_RATE = 0.02
VECTOR_RATE = 0.01
CLIP_NORM = 1.0
ADAM_EPS = 1e-08


def passed_along(value, axis, steps):
    count = lax.axis_size(axis)
    first, last = (max(0, -steps), min(count, count - steps))
    return lax.ppermute(value, axis, [(source, source + steps) for source in range(first, last)])


def entering(value, axis, join, neutral):
    count, mine = (lax.axis_size(axis), lax.axis_index(axis))
    pieces = jax.tree.map(lambda part: lax.all_gather(part, axis), value)
    running = jax.tree.map(
        lambda part, zero: jnp.full_like(part, 0) + jnp.asarray(zero, part.dtype), value, neutral
    )

    def entering_hop(position, running):
        longer = join(running, jax.tree.map(lambda part: part[position], pieces))
        return jax.tree.map(lambda new, old: jnp.where(position < mine, new, old), longer, running)

    return lax.fori_loop(0, count - 1, entering_hop, running)


def prefix_2(value, axis, combine, identity):
    count, index = (lax.axis_size(axis), lax.axis_index(axis))
    everything = jax.tree.map(
        lambda part, kind: lax.all_gather(part.astype(kind), axis),
        value,
        jax.tree.map(lambda a: jnp.bfloat16 if a.dtype == jnp.float32 else a.dtype, value),
    )
    start = jax.tree.map(
        lambda part, zero: jnp.broadcast_to(jnp.asarray(zero, part.dtype), part.shape),
        value,
        identity,
    )

    def prefix_hop(k, before):
        at = count - 1 - k
        reached = at > index
        new = combine(
            before, jax.tree.map(lambda part, own: part[at].astype(own.dtype), everything, value)
        )
        return jax.tree.map(lambda a, b: jnp.where(reached, a, b), new, before)

    return lax.fori_loop(0, count, prefix_hop, start)


def unpack_vectors(vectors):
    widths = [2 * H * D, KCONV * (2 * H * DKH + H * DVH), D, D, DVH, H, H]
    pieces = []
    offset = 0
    for span_width in widths:
        pieces.append(vectors[offset : offset + span_width])
        offset += span_width
    projection = pieces[0].reshape(2 * H, D)
    conv_taps = pieces[1].reshape(KCONV, 2 * H * DKH + H * DVH)
    return (projection, conv_taps, pieces[2], pieces[3], pieces[4], pieces[5], pieces[6])


def rms_scale(values, gain):
    inverse = lax.rsqrt(jnp.mean(values * values, axis=-1, keepdims=True) + RMS_EPS)
    return values * inverse * gain


def swiglu(values):
    return jax.nn.silu(values[:, :FF]) * values[:, FF:]


def contract_last(left, right):
    return lax.dot_general(
        left, right, (((1,), (1,)), ((), ())), preferred_element_type=jnp.float32
    )


def contract_first(left, right):
    return lax.dot_general(
        left, right, (((0,), (0,)), ((), ())), preferred_element_type=jnp.float32
    )


def short_conv(extended, extended_ids, tap_weights):
    out_rows = extended.shape[0] - (KCONV - 1)
    current_ids = extended_ids[KCONV - 1 :]
    summed = jnp.zeros((out_rows, extended.shape[1]), jnp.float32)
    for tap_index in range(KCONV):
        same_document = (extended_ids[tap_index : tap_index + out_rows] == current_ids).astype(
            jnp.float32
        )
        summed = (
            summed
            + tap_weights[tap_index]
            * extended[tap_index : tap_index + out_rows]
            * same_document[:, None]
        )
    return jax.nn.silu(summed)


def delta_block(carry_state, block_inputs):
    queries, keys_unit, values, beta_rates, log_decay, block_ids, before_id = block_inputs
    length_block = block_ids.shape[0]
    cumulative = jnp.cumsum(log_decay, axis=0).T
    row_index = lax.broadcasted_iota(jnp.int32, (length_block, length_block), 0)
    col_index = lax.broadcasted_iota(jnp.int32, (length_block, length_block), 1)
    linked = (row_index >= col_index) & (block_ids[:, None] == block_ids[None, :])
    spread = cumulative[:, :, None] - cumulative[:, None, :]
    ratios = jnp.where(linked[None], jnp.exp(jnp.where(linked[None], spread, 0.0)), 0.0)
    carried = jnp.exp(cumulative) * (block_ids == before_id).astype(jnp.float32)[None, :]
    beta_heads = beta_rates.T
    key_gram = jnp.einsum("thd,shd->hts", keys_unit, keys_unit, precision=PRECISE)
    cross_gram = jnp.einsum("thd,shd->hts", queries, keys_unit, precision=PRECISE)
    strict = jnp.where((row_index > col_index)[None], ratios * key_gram, 0.0)
    system = jnp.eye(length_block, dtype=jnp.float32)[None] + beta_heads[:, :, None] * strict
    key_state = jnp.einsum("thd,hdw->htw", keys_unit, carry_state, precision=PRECISE)
    value_heads = jnp.transpose(values, (1, 0, 2))
    target = beta_heads[:, :, None] * (value_heads - carried[:, :, None] * key_state)
    solved = jax.scipy.linalg.solve_triangular(system, target, lower=True, unit_diagonal=True)
    query_state = jnp.einsum("thd,hdw->htw", queries, carry_state, precision=PRECISE)
    outputs = carried[:, :, None] * query_state + jnp.einsum(
        "hts,hsw->htw", ratios * cross_gram, solved, precision=PRECISE
    )
    last_ratios = ratios[:, length_block - 1, :]
    new_state = carried[:, length_block - 1][:, None, None] * carry_state + jnp.einsum(
        "shd,hs,hsw->hdw", keys_unit, last_ratios, solved, precision=PRECISE
    )
    return (new_state, jnp.transpose(outputs, (1, 0, 2)))


def mixer_core(
    extended,
    extended_ids,
    normed_in,
    tap_weights,
    small_weights,
    decay_log,
    decay_bias,
    start_state,
    first_id,
):
    count_rows = normed_in.shape[0]
    conv_out = short_conv(extended, extended_ids, tap_weights)
    small = jnp.dot(normed_in, small_weights.T, precision=PRECISE)
    beta_rates = jax.nn.sigmoid(small[:, :H])
    log_decay = -jnp.exp(decay_log) * jax.nn.softplus(small[:, H:] + decay_bias)
    queries = conv_out[:, : H * DKH].reshape(count_rows, H, DKH)
    queries = (
        queries
        * lax.rsqrt(jnp.sum(queries * queries, axis=-1, keepdims=True) + RMS_EPS)
        * DKH ** (-0.5)
    )
    keys_unit = conv_out[:, H * DKH : 2 * H * DKH].reshape(count_rows, H, DKH)
    keys_unit = keys_unit * lax.rsqrt(
        jnp.sum(keys_unit * keys_unit, axis=-1, keepdims=True) + RMS_EPS
    )
    values = conv_out[:, 2 * H * DKH :].reshape(count_rows, H, DVH)
    extra_width = start_state.shape[2] - DVH
    values = jnp.concatenate([values, jnp.zeros((count_rows, H, extra_width), jnp.float32)], axis=2)
    blocks = count_rows // STRETCH
    row_ids = extended_ids[KCONV - 1 :].reshape(blocks, STRETCH)
    before_ids = jnp.concatenate([jnp.reshape(first_id, (1,)), row_ids[: blocks - 1, STRETCH - 1]])
    final_state, outputs = lax.scan(
        jax.checkpoint(delta_block),
        start_state,
        (
            queries.reshape(blocks, STRETCH, H, DKH),
            keys_unit.reshape(blocks, STRETCH, H, DKH),
            values.reshape(blocks, STRETCH, H, start_state.shape[2]),
            beta_rates.reshape(blocks, STRETCH, H),
            log_decay.reshape(blocks, STRETCH, H),
            row_ids,
            before_ids,
        ),
    )
    return (outputs.reshape(count_rows, H, start_state.shape[2]), final_state)


def compose_maps(earlier, later):
    return (
        jnp.einsum("hij,hjk->hik", later[0], earlier[0], precision=PRECISE),
        jnp.einsum("hij,hjw->hiw", later[0], earlier[1], precision=PRECISE) + later[1],
    )


def muon_update(block_rows, gram, total_rows):
    inverse_norm = 1.0 / (jnp.sqrt(jnp.trace(gram)) + 1e-07)
    current = gram * (inverse_norm * inverse_norm)
    identity = jnp.eye(gram.shape[0], dtype=jnp.float32)
    ortho = block_rows * inverse_norm
    for iteration in range(NS_ITERS):
        square = jnp.dot(current, current, precision=PRECISE)
        factor = NS_A * identity + NS_B * current + NS_C * square
        ortho = jnp.dot(ortho, factor, precision=PRECISE)
        if iteration + 1 < NS_ITERS:
            current = jnp.dot(
                current, jnp.dot(factor, factor, precision=PRECISE), precision=PRECISE
            )
    return -LEARN_RATE * 0.2 * math.sqrt(max(total_rows, D)) * ortho


def self_gram(matrix):
    return lax.dot_general(matrix, matrix, (((0,), (0,)), ((), ())), precision=PRECISE)


def shards(
    tokens,
    cotangent,
    segments,
    weight_in,
    weight_out,
    weight_up,
    weight_down,
    vectors,
    momentum_in,
    momentum_out,
    momentum_up,
    momentum_down,
    first_moment,
    second_moment,
):
    projection, conv_taps, gain_one, gain_two, gain_head, decay_log, decay_bias = unpack_vectors(
        vectors
    )
    full_in, full_out, full_up, full_down = (
        lax.all_gather(weight_in.astype(jnp.bfloat16), "fsdp", axis=0, tiled=True),
        lax.all_gather(weight_out.astype(jnp.bfloat16), "fsdp", axis=0, tiled=True),
        lax.all_gather(weight_up.astype(jnp.bfloat16), "fsdp", axis=0, tiled=True),
        lax.all_gather(weight_down.astype(jnp.bfloat16), "fsdp", axis=0, tiled=True),
    )
    token_rows = tokens[0].astype(jnp.float32)
    count_rows = token_rows.shape[0]
    conv_width = 2 * H * DKH + H * DVH
    id_plus = segments[0].astype(jnp.float32) + 1.0
    normed, norm_back = jax.vjp(rms_scale, token_rows, gain_one)
    normed_low = normed.astype(jnp.bfloat16)
    projected = contract_last(normed_low, full_in).astype(jnp.bfloat16)
    conv_low = projected[:, :conv_width]
    gate_low = projected[:, conv_width:]
    edge_rows, edge_ids = passed_along(
        (
            conv_low[count_rows - KCONV + 1 :],
            id_plus[count_rows - KCONV + 1 :].astype(jnp.bfloat16),
        ),
        "seq",
        1,
    )
    extended_ids = jnp.concatenate([edge_ids.astype(jnp.float32), id_plus])
    extended = jnp.concatenate([edge_rows, conv_low], axis=0).astype(jnp.float32)
    identity = jnp.broadcast_to(jnp.eye(DKH, dtype=jnp.float32), (H, DKH, DKH))
    zero_state = jnp.zeros((H, DKH, DVH), jnp.float32)
    start_state = jnp.concatenate([zero_state, identity], axis=2)

    def mixer_local(conv_values, normed_values, tap_weights, small_weights, rates, rate_bias):
        return mixer_core(
            conv_values,
            extended_ids,
            normed_values,
            tap_weights,
            small_weights,
            rates,
            rate_bias,
            start_state,
            extended_ids[KCONV - 2],
        )

    (local_out, final_state), mixer_back = jax.vjp(
        mixer_local,
        extended,
        normed_low.astype(jnp.float32),
        conv_taps,
        projection,
        decay_log,
        decay_bias,
    )
    own_part = local_out[:, :, :DVH]
    reach_rows = local_out[:, :, DVH:]
    carry_state = final_state[:, :, :DVH]
    transfer = final_state[:, :, DVH:]
    prefix = entering((transfer, carry_state), "seq", compose_maps, (identity, zero_state))
    state_in = prefix[1]
    recurrent = own_part + jnp.einsum("thi,hiw->thw", reach_rows, state_in, precision=PRECISE)

    def gate_local(recurrent_values, gate_values, head_gain):
        return rms_scale(recurrent_values, head_gain).reshape(count_rows, H * DVH) * jax.nn.silu(
            gate_values
        )

    gated, gate_back = jax.vjp(gate_local, recurrent, gate_low.astype(jnp.float32), gain_head)
    gated_low = gated.astype(jnp.bfloat16)
    attention = jnp.dot(gated_low, full_out, preferred_element_type=jnp.float32)
    residual = token_rows + attention
    normed_two, norm_two_back = jax.vjp(rms_scale, residual, gain_two)
    normed_two_low = normed_two.astype(jnp.bfloat16)
    gate_up = contract_last(normed_two_low, full_up)
    hidden, swiglu_back = jax.vjp(swiglu, gate_up)
    hidden_low = hidden.astype(jnp.bfloat16)
    feed_out = jnp.dot(hidden_low, full_down, preferred_element_type=jnp.float32)
    mixed = (residual + feed_out).astype(jnp.bfloat16)[None]
    back_in, back_out, back_up, back_down = (full_in, full_out, full_up, full_down)
    grad_rows = cotangent[0].astype(jnp.float32)
    grad_feed_low = cotangent[0]
    grad_down = contract_first(hidden_low, grad_feed_low)
    grad_hidden = contract_last(grad_feed_low, back_down)
    (grad_gate_up,) = swiglu_back(grad_hidden)
    grad_gate_up_low = grad_gate_up.astype(jnp.bfloat16)
    grad_up = contract_first(grad_gate_up_low, normed_two_low)
    grad_normed_two = jnp.dot(grad_gate_up_low, back_up, preferred_element_type=jnp.float32)
    grad_resid_part, grad_gain_two = norm_two_back(grad_normed_two)
    grad_residual = grad_rows + grad_resid_part
    grad_attn_low = grad_residual.astype(jnp.bfloat16)
    grad_wout = contract_first(gated_low, grad_attn_low)
    grad_gated = contract_last(grad_attn_low, back_out)
    grad_recurrent, grad_gate_in, grad_gain_head = gate_back(grad_gated)
    grad_state_local = jnp.einsum("thi,thw->hiw", reach_rows, grad_recurrent, precision=PRECISE)
    grad_reach = jnp.einsum("thw,hiw->thi", grad_recurrent, state_in, precision=PRECISE)
    back_prefix = prefix_2(
        (jnp.swapaxes(transfer, 1, 2), grad_state_local),
        "seq",
        compose_maps,
        (identity, zero_state),
    )
    grad_after = back_prefix[1]
    grad_transfer = jnp.einsum("hiw,hjw->hij", grad_after, state_in, precision=PRECISE)
    grad_outputs = jnp.concatenate([grad_recurrent, grad_reach], axis=2)
    grad_final = jnp.concatenate([grad_after, grad_transfer], axis=2)
    (
        grad_extended,
        grad_normed_small,
        grad_taps,
        grad_projection,
        grad_decay_log,
        grad_decay_bias,
    ) = mixer_back((grad_outputs, grad_final))
    from_next = passed_along(grad_extended[: KCONV - 1].astype(jnp.bfloat16), "seq", -1).astype(
        jnp.float32
    )
    grad_conv = grad_extended[KCONV - 1 :]
    grad_conv = jnp.concatenate(
        [grad_conv[: count_rows - KCONV + 1], grad_conv[count_rows - KCONV + 1 :] + from_next],
        axis=0,
    )
    grad_projected_low = jnp.concatenate([grad_conv, grad_gate_in], axis=1).astype(jnp.bfloat16)
    grad_win = contract_first(grad_projected_low, normed_low)
    grad_normed = (
        jnp.dot(grad_projected_low, back_in, preferred_element_type=jnp.float32) + grad_normed_small
    )
    grad_token_part, grad_gain_one = norm_back(grad_normed)
    grad_tokens = (grad_residual + grad_token_part)[None]
    reduced_in, reduced_out, reduced_up, reduced_down = (
        lax.psum_scatter(grad_win, ("seq", "fsdp"), scatter_dimension=0, tiled=True),
        lax.psum_scatter(grad_wout, ("seq", "fsdp"), scatter_dimension=0, tiled=True),
        lax.psum_scatter(grad_up, ("seq", "fsdp"), scatter_dimension=0, tiled=True),
        lax.psum_scatter(grad_down, ("seq", "fsdp"), scatter_dimension=0, tiled=True),
    )
    grad_vector_part = jnp.concatenate(
        [
            grad_projection.reshape(-1),
            grad_taps.reshape(-1),
            grad_gain_one,
            grad_gain_two,
            grad_gain_head,
            grad_decay_log,
            grad_decay_bias,
        ]
    )
    squares_local = (
        jnp.sum(reduced_in * reduced_in)
        + jnp.sum(reduced_out * reduced_out)
        + jnp.sum(reduced_up * reduced_up)
        + jnp.sum(reduced_down * reduced_down)
    )
    grad_vector, squares_total = lax.psum((grad_vector_part, squares_local), ("seq", "fsdp"))
    grad_norm = jnp.sqrt(squares_total + jnp.sum(grad_vector * grad_vector))
    clipping = jnp.minimum(1.0, CLIP_NORM / (grad_norm + 1e-06))
    renewed_in = MOMENTUM * momentum_in + (1.0 - MOMENTUM) * clipping * reduced_in
    renewed_out = MOMENTUM * momentum_out + (1.0 - MOMENTUM) * clipping * reduced_out
    renewed_up = MOMENTUM * momentum_up + (1.0 - MOMENTUM) * clipping * reduced_up
    renewed_down = MOMENTUM * momentum_down + (1.0 - MOMENTUM) * clipping * reduced_down
    gram_in, gram_out, gram_up, gram_down = lax.psum(
        (
            self_gram(renewed_in),
            self_gram(renewed_out),
            self_gram(renewed_up),
            self_gram(renewed_down),
        ),
        ("seq", "fsdp"),
    )
    devices_all = lax.axis_size(("seq", "fsdp"))
    update_in = muon_update(renewed_in, gram_in, renewed_in.shape[0] * devices_all)
    update_out = muon_update(renewed_out, gram_out, renewed_out.shape[0] * devices_all)
    update_up = muon_update(renewed_up, gram_up, renewed_up.shape[0] * devices_all)
    update_down = muon_update(renewed_down, gram_down, renewed_down.shape[0] * devices_all)
    clipped = clipping * grad_vector
    first_next = ADAM_ONE * first_moment + (1.0 - ADAM_ONE) * clipped
    second_next = ADAM_TWO * second_moment + (1.0 - ADAM_TWO) * clipped * clipped
    update_vector = (
        -VECTOR_RATE
        * (first_next / (1.0 - ADAM_ONE**STEP))
        / (jnp.sqrt(second_next / (1.0 - ADAM_TWO**STEP)) + ADAM_EPS)
    )
    return (
        mixed,
        grad_tokens,
        reduced_in,
        reduced_out,
        reduced_up,
        reduced_down,
        renewed_in,
        renewed_out,
        renewed_up,
        renewed_down,
        update_in,
        update_out,
        update_up,
        update_down,
        grad_vector,
        first_next,
        second_next,
        update_vector,
        grad_norm.reshape(1),
    )


def permuted(value, axis, bit):
    count = lax.axis_size(axis)
    return lax.ppermute(value, axis, [(i, i ^ (1 << bit)) for i in range(count)])


def picked(value, index, position=0):
    return lax.dynamic_index_in_dim(value, index, position, keepdims=False)


def scattered_sum(parts, axis, order, wire=jnp.bfloat16):
    width = len(order)
    mine = lax.axis_index(axis)
    held = parts.reshape((2,) * width + parts.shape[1:])
    left = list(range(width - 1, -1, -1))
    for bit in order:
        position = left.index(bit)
        value = (mine >> bit) & 1
        keep = picked(held, value, position)
        gone = picked(held, 1 - value, position)
        held = keep.astype(jnp.float32) + permuted(gone.astype(wire), axis, bit).astype(jnp.float32)
        left.remove(bit)
    return held


def gathered(value, axis, order):
    mine = lax.axis_index(axis)
    held = value[None]
    done = []
    for bit in order:
        other = permuted(held, axis, bit)
        high = ((mine >> bit) & 1) == 1
        first = jnp.where(high, other, held)
        second = jnp.where(high, held, other)
        joined = jnp.stack([first, second])
        place = sum(1 for d in done if d > bit)
        shape = (2,) * (len(done) + 1) + value.shape
        joined = jnp.moveaxis(joined.reshape(shape), 0, place)
        done = sorted(done + [bit], reverse=True)
        held = joined.reshape((2 ** len(done),) + value.shape)
    return held


def summed_everywhere(value, axes_bits):
    for axis, bit in axes_bits:
        value = value + permuted(value, axis, bit)
    return value


def matchings(targets, slots, count):
    remaining = {src: [(dst, i) for i, (dst, _) in enumerate(targets[src])] for src in range(count)}
    rounds = []
    for _ in range(slots):
        owner = {}

        def seek(src, seen):
            for dst, i in remaining[src]:
                if dst in seen:
                    continue
                seen.add(dst)
                if dst not in owner or seek(owner[dst][0], seen):
                    owner[dst] = (src, i)
                    return True
            return False

        for src in range(count):
            assert seek(src, set())
        chosen = {}
        for dst, (src, i) in owner.items():
            chosen[src] = (dst, i)
        for src, (dst, i) in chosen.items():
            remaining[src].remove((dst, i))
        rounds.append(chosen)
    return rounds


def routed(granules, targets, axes, me):
    slots, count = (len(targets[0]), len(targets))
    pieces = []
    for chosen in matchings(targets, slots, count):
        sent = jnp.asarray([chosen[src][1] for src in range(count)], jnp.int32)
        landing = [0] * count
        for src, (dst, i) in chosen.items():
            landing[dst] = targets[src][i][1]
        piece = lax.ppermute(
            picked(granules, sent[me]), axes, [(src, chosen[src][0]) for src in range(count)]
        )
        pieces.append((piece, jnp.asarray(landing, jnp.int32)[me]))
    return [
        sum(
            jnp.where(place == slot, piece.astype(jnp.float32), 0.0)
            for piece, place in pieces
        )
        for slot in range(slots)
    ]


CHUNK = 128
MIX = lax.Precision.HIGH


def product(spec, left, right):
    return jnp.einsum(spec, left, right, precision=MIX, preferred_element_type=jnp.float32)


def unit_inverse(strict):
    size = strict.shape[-1]
    rows = lax.broadcasted_iota(jnp.int32, (size, size), 0)
    cols = lax.broadcasted_iota(jnp.int32, (size, size), 1)
    exact = lambda a, b: jnp.einsum("nij,njk->nik", a, b, precision=PRECISE)
    eye = (rows == cols).astype(jnp.float32)[None]
    base = -jnp.where((rows // 8 == cols // 8)[None], strict, 0.0)
    second = exact(base, base)
    fourth = exact(second, second)
    inverse = eye + base
    inverse = inverse + exact(inverse, second)
    inverse = inverse + exact(inverse, fourth)
    width = 8
    while width < size:
        joint = (rows // (2 * width) == cols // (2 * width)) & (rows // width != cols // width)
        inverse = inverse - exact(exact(inverse, jnp.where(joint[None], strict, 0.0)), inverse)
        width *= 2
    return inverse


@jax.custom_vjp
def solved_with(strict, right):
    return product("nij,njw->niw", unit_inverse(strict), right)


def solved_keep(strict, right):
    inverse = unit_inverse(strict)
    answer = product("nij,njw->niw", inverse, right)
    return answer, (inverse, answer)


def solved_back(kept, grad):
    inverse, answer = kept
    grad_right = product("nji,njw->niw", inverse, grad)
    return -product("niw,njw->nij", grad_right, answer), grad_right


solved_with.defvjp(solved_keep, solved_back)


def chunk_maps(queries, keys, values, beta, cumulative, linked, below, first_open):
    spread = cumulative[:, :, None] - cumulative[:, None, :]
    ratios = jnp.where(linked, jnp.exp(jnp.where(linked, spread, 0.0)), 0.0)
    carried = jnp.exp(cumulative) * first_open
    key_gram = product("ntd,nsd->nts", keys, keys)
    cross = ratios * product("ntd,nsd->nts", queries, keys)
    strict = beta[:, :, None] * jnp.where(below, ratios * key_gram, 0.0)
    right = beta[:, :, None] * jnp.concatenate([carried[:, :, None] * keys, values], axis=2)
    both = solved_with(strict, right)
    weighted = keys * ratios[:, -1, :, None]
    onward = product("nsd,nsw->ndw", weighted, both)
    outward = product("nts,nsw->ntw", cross, both)
    size = keys.shape[2]
    eye = jnp.eye(size, dtype=jnp.float32)[None]
    state_map = carried[:, -1][:, None, None] * eye - onward[:, :, :size]
    reach = carried[:, :, None] * queries - outward[:, :, :size]
    return state_map, onward[:, :, size:], reach, outward[:, :, size:]


def pair_inputs(conv_in, small, ids, taps, rate, bias):
    count = conv_in.shape[0]
    extended = jnp.concatenate([jnp.zeros((KCONV - 1, conv_in.shape[1]), jnp.float32), conv_in])
    extended_ids = jnp.concatenate([jnp.zeros((KCONV - 1,), jnp.float32), ids])
    conv_out = short_conv(extended, extended_ids, taps)
    beta = jax.nn.sigmoid(small[:, 0])
    log_decay = -jnp.exp(rate) * jax.nn.softplus(small[:, 1] + bias)
    queries = conv_out[:, :DKH]
    queries = (
        queries
        * lax.rsqrt(jnp.sum(queries * queries, axis=-1, keepdims=True) + RMS_EPS)
        * DKH ** (-0.5)
    )
    keys = conv_out[:, DKH : 2 * DKH]
    keys = keys * lax.rsqrt(jnp.sum(keys * keys, axis=-1, keepdims=True) + RMS_EPS)
    chunks = count // CHUNK
    cut = lambda a: a.reshape((chunks, CHUNK) + a.shape[1:])
    cumulative = jnp.cumsum(cut(log_decay), axis=1)
    return cut(queries), cut(keys), cut(conv_out[:, 2 * DKH :]), cut(beta), cumulative


def pair_masks(ids):
    chunks = ids.shape[0] // CHUNK
    cut = ids.reshape(chunks, CHUNK)
    rows = lax.broadcasted_iota(jnp.int32, (CHUNK, CHUNK), 0)
    cols = lax.broadcasted_iota(jnp.int32, (CHUNK, CHUNK), 1)
    linked = (rows >= cols)[None] & (cut[:, :, None] == cut[:, None, :])
    before = jnp.concatenate([jnp.zeros((1,), ids.dtype), cut[:-1, -1]])
    return linked, (rows > cols)[None], (cut == before[:, None]).astype(jnp.float32)


def states_forward(state_map, addend):
    state = jnp.zeros(addend.shape[1:], jnp.float32)
    entering_states = []
    for n in range(addend.shape[0]):
        entering_states.append(state)
        state = jnp.dot(state_map[n], state, precision=MIX) + addend[n]
    return jnp.stack(entering_states)


def states_backward(state_map, grad_entering):
    grad = jnp.zeros(grad_entering.shape[1:], jnp.float32)
    after = []
    for n in reversed(range(grad_entering.shape[0])):
        after.append(grad)
        grad = grad_entering[n] + jnp.einsum("ij,iw->jw", state_map[n], grad, precision=MIX)
    return jnp.stack(after[::-1])


def gram_panels(matrix):
    side = D // 4
    narrow = matrix.astype(jnp.bfloat16)
    blocks = []
    for i in range(4):
        panel = contract_first(narrow[:, i * side : (i + 1) * side], narrow[:, i * side :])
        for j in range(4 - i):
            blocks.append(panel[:, j * side : (j + 1) * side])
    return blocks


def gram_whole(blocks):
    index = {}
    count = 0
    for i in range(4):
        for j in range(i, 4):
            index[i, j] = count
            count += 1
    rows = [
        jnp.concatenate(
            [blocks[index[i, j]] if i <= j else blocks[index[j, i]].T for j in range(4)], axis=1
        )
        for i in range(4)
    ]
    return jnp.concatenate(rows, axis=0)


def thin_update(block_rows, gram, total_rows):
    inverse_norm = 1.0 / (jnp.sqrt(jnp.trace(gram.astype(jnp.float32))) + 1e-07)
    current = (gram.astype(jnp.float32) * (inverse_norm * inverse_norm)).astype(jnp.bfloat16)

    def times(rows):
        return jnp.dot(rows.astype(jnp.bfloat16), current, preferred_element_type=jnp.float32)

    def through(rows):
        once = times(rows)
        return NS_A * rows + NS_B * once + NS_C * times(once)

    def advanced(rows):
        return through(through(times(rows)))

    first = through(block_rows * inverse_norm)
    once = advanced(first)
    ortho = NS_A * first + NS_B * once + NS_C * advanced(once)
    return -LEARN_RATE * 0.2 * math.sqrt(max(total_rows, D)) * ortho


def head_tables(fsdp):
    per = (2 * H * DKH + 2 * H * DVH) // fsdp // DKH
    give, find = ([], [])
    for head in range(H):
        wanted = [head, H + head] + [
            2 * H + base + 2 * head + k for base in (0, 2 * H) for k in range(2)
        ]
        lists = [[g % per for g in wanted if g // per == f] for f in range(fsdp)]
        seen = [0] * fsdp
        where = []
        for g in wanted:
            f = g // per
            where.append((f, seen[f]))
            seen[f] += 1
        most = 2
        assert max(len(one) for one in lists) <= most
        give.append([one + [0] * (most - len(one)) for one in lists])
        find.append([f * most + j for f, j in where])
    return give, find


def in_targets(seq, fsdp):
    granule = 64
    per = (2 * H * DKH + 2 * H * DVH) // (seq * fsdp) // granule
    targets = []
    for s in range(seq):
        rows = []
        for start, size in (
            (s * DKH, DKH),
            (H * DKH + s * DKH, DKH),
            (2 * H * DKH + s * DVH, DVH),
            (2 * H * DKH + H * DVH + s * DVH, DVH),
        ):
            rows += [start // granule + k for k in range(size // granule)]
        for f in range(fsdp):
            own = rows[f * per : (f + 1) * per]
            targets.append([(g // per, g % per) for g in own])
    return targets


def up_targets(seq, fsdp):
    piece = FF // (seq * fsdp)
    return [
        [((f * seq + s) // 2, (f * seq + s) % 2), (seq * fsdp // 2 + (f * seq + s) // 2, (f * seq + s) % 2)]
        for s in range(seq)
        for f in range(fsdp)
    ]


def down_targets(seq, fsdp):
    return [[(f * seq + s, 0)] for s in range(seq) for f in range(fsdp)]


def up_shuffle_targets(fsdp):
    half = fsdp // 2
    return [[(2 * (f % half) + k, f // half) for k in range(2)] for f in range(fsdp)]


def pair_shards(
    tokens,
    cotangent,
    segments,
    weight_in,
    weight_out,
    weight_up,
    weight_down,
    vectors,
    momentum_in,
    momentum_out,
    momentum_up,
    momentum_down,
    first_moment,
    second_moment,
):
    seq, fsdp = (lax.axis_size("seq"), lax.axis_size("fsdp"))
    head, group = (lax.axis_index("seq"), lax.axis_index("fsdp"))
    me = head * fsdp + group
    seq_bits, fsdp_bits = (seq.bit_length() - 1, fsdp.bit_length() - 1)
    fsdp_order = list(range(fsdp_bits))
    projection, conv_taps, gain_one, gain_two, gain_head, decay_log, decay_bias = unpack_vectors(
        vectors
    )
    own = tokens.shape[1]
    length = own * seq
    heads_low = jnp.bfloat16

    row_ids = jnp.zeros((16, D), heads_low)
    row_ids = row_ids.at[0, :own].set((segments[0] + 1).astype(heads_low))
    packed = lax.all_gather(jnp.concatenate([tokens[0], row_ids]), "seq")
    token_seq = packed[:, :own].reshape(length, D)
    ids = packed[:, own, :own].reshape(length).astype(jnp.float32)

    give, find = head_tables(fsdp)
    give_table = jnp.asarray(give, jnp.int32)
    find_table = jnp.asarray(find, jnp.int32)
    slices = [
        lax.dynamic_slice_in_dim(weight_in, give_table[head, group, j] * DKH, DKH, 0)
        for j in range(2)
    ]
    given = lax.all_gather(jnp.stack(slices).astype(heads_low), "fsdp", axis=0, tiled=True)
    head_rows = jnp.concatenate([picked(given, find_table[head, j]) for j in range(6)])
    small_rows = jnp.stack([picked(projection, head), picked(projection, H + head)])
    taps_rows = conv_taps.reshape(KCONV, 4 * H, DKH)
    taps_head = jnp.concatenate(
        [
            picked(taps_rows, head, 1),
            picked(taps_rows, H + head, 1),
            picked(taps_rows, 2 * H + 2 * head, 1),
            picked(taps_rows, 2 * H + 2 * head + 1, 1),
        ],
        axis=1,
    )
    rate, bias = (decay_log[head], decay_bias[head])

    full_out = lax.all_gather(weight_out.astype(heads_low), "fsdp", axis=0, tiled=True)
    cot_group = gathered(cotangent[0], "fsdp", fsdp_order[::-1]).reshape(fsdp * own, D)
    half_up = weight_up.shape[0] // 2
    up_gate, up_value = [
        part.astype(heads_low)
        for part in routed(
            weight_up.astype(heads_low).reshape(2, half_up, D), up_shuffle_targets(fsdp), "fsdp", group
        )
    ]
    low_up = jnp.concatenate([up_gate, up_value])
    low_down = weight_down.astype(heads_low)

    token_rows = token_seq.astype(jnp.float32)
    normed_low = rms_scale(token_rows, gain_one).astype(heads_low)
    projected = contract_last(normed_low, head_rows).astype(heads_low)
    conv_in = projected[:, : 2 * DKH + DVH].astype(jnp.float32)
    gate_in = projected[:, 2 * DKH + DVH :].astype(jnp.float32)
    small = lax.dot_general(
        normed_low.astype(jnp.float32), small_rows, (((1,), (1,)), ((), ())), precision=PRECISE
    )
    linked, below, first_open = pair_masks(ids)
    parts, inputs_back = jax.vjp(
        lambda c, m, t, r, b: pair_inputs(c, m, ids, t, r, b),
        conv_in,
        small,
        taps_head,
        rate,
        bias,
    )
    maps, maps_back = jax.vjp(
        lambda q, k, v, b, c: chunk_maps(q, k, v, b, c, linked, below, first_open), *parts
    )
    state_map, addend, reach, local = maps
    states = states_forward(state_map, addend)
    recurrent = (product("ntd,ndw->ntw", reach, states) + local).reshape(length, DVH)

    def gate_pair(recurrent_values, gate_values, head_gain):
        return rms_scale(recurrent_values, head_gain) * jax.nn.silu(gate_values)

    gated, gate_back = jax.vjp(gate_pair, recurrent, gate_in, gain_head)
    gated_low = gated.astype(heads_low)
    gated_own = lax.all_to_all(gated_low.reshape(seq, own, DVH), "seq", 0, 0)
    gated_own = jnp.transpose(gated_own, (1, 0, 2)).reshape(own, H * DVH)

    own_rows = tokens[0].astype(jnp.float32)
    residual = own_rows + jnp.dot(gated_own, full_out, preferred_element_type=jnp.float32)
    normed_two, norm_two_back = jax.vjp(rms_scale, residual, gain_two)
    two_group = gathered(normed_two.astype(heads_low), "fsdp", fsdp_order[::-1])
    two_group = two_group.reshape(fsdp * own, D)
    gate_up = contract_last(two_group, low_up)
    units = half_up

    def swiglu_own(values):
        return jax.nn.silu(values[:, :units]) * values[:, units:]

    hidden, swiglu_back = jax.vjp(swiglu_own, gate_up)
    hidden_low = hidden.astype(heads_low)
    feed_parts = jnp.dot(hidden_low, low_down, preferred_element_type=jnp.float32)
    feed_out = scattered_sum(feed_parts.reshape(fsdp, own, D), "fsdp", fsdp_order)
    mixed = (residual + feed_out).astype(heads_low)[None]

    grad_hidden = contract_last(cot_group, low_down)
    (grad_gate_up,) = swiglu_back(grad_hidden)
    grad_gate_up_low = grad_gate_up.astype(heads_low)
    two_parts = jnp.dot(grad_gate_up_low, low_up, preferred_element_type=jnp.float32)
    grad_normed_two = scattered_sum(two_parts.reshape(fsdp, own, D), "fsdp", fsdp_order)
    grad_down_part = contract_first(hidden_low, cot_group)
    grad_up_part = contract_first(grad_gate_up_low, two_group)
    grad_resid_part, grad_gain_two = norm_two_back(grad_normed_two)
    grad_residual = cotangent[0].astype(jnp.float32) + grad_resid_part
    grad_attn_low = grad_residual.astype(heads_low)
    attn_seq = lax.all_gather(grad_attn_low, "seq", axis=0, tiled=True)

    piece = FF // (seq * fsdp)
    ff_parts = jnp.concatenate(
        [
            grad_down_part.reshape(seq, 1, piece, D),
            jnp.transpose(grad_up_part.reshape(2, seq, piece, D), (1, 0, 2, 3)),
        ],
        axis=1,
    )
    ff_low = ff_parts.astype(heads_low)
    ff_left = scattered_sum(ff_low[..., : D // 2], "seq", [0, 1, 2])
    ff_right = scattered_sum(ff_low[..., D // 2 :], "seq", [1, 0, 2])
    ff_own = jnp.concatenate([ff_left, ff_right], axis=-1).astype(heads_low)
    both = ("seq", "fsdp")
    (reduced_down,) = routed(ff_own[:1], down_targets(seq, fsdp), both, me)
    reduced_up = jnp.concatenate(routed(ff_own[1:], up_targets(seq, fsdp), both, me))

    out_rows = lax.dynamic_slice_in_dim(full_out, head * DVH, DVH, 0)
    grad_gated = contract_last(attn_seq, out_rows)
    grad_out_part = contract_first(gated_low, attn_seq)
    reduced_out = scattered_sum(grad_out_part.reshape(fsdp, DVH // fsdp, D), "fsdp", fsdp_order)
    grad_recurrent, grad_gate_in, grad_gain_head = gate_back(grad_gated)
    grad_out_chunks = grad_recurrent.reshape(local.shape)
    grad_entering = product("ntd,ntw->ndw", reach, grad_out_chunks)
    grad_after = states_backward(state_map, grad_entering)
    grad_maps = (
        product("niw,njw->nij", grad_after, states),
        grad_after,
        product("ntw,ndw->ntd", grad_out_chunks, states),
        grad_out_chunks,
    )
    grad_conv, grad_small, grad_taps, grad_rate, grad_bias = inputs_back(maps_back(grad_maps))
    grad_projected_low = jnp.concatenate([grad_conv, grad_gate_in], axis=1).astype(heads_low)
    grad_in_part = contract_first(grad_projected_low, normed_low)
    normed_parts = jnp.dot(grad_projected_low, head_rows, preferred_element_type=jnp.float32)
    normed_parts = normed_parts + jnp.dot(grad_small, small_rows, precision=PRECISE)
    normed_low_parts = normed_parts.astype(heads_low).reshape(seq, own, D)
    normed_left = scattered_sum(normed_low_parts[..., : D // 2], "seq", [0, 1, 2])
    normed_right = scattered_sum(normed_low_parts[..., D // 2 :], "seq", [1, 0, 2])
    grad_normed = jnp.concatenate([normed_left, normed_right], axis=-1)
    _, norm_back = jax.vjp(rms_scale, own_rows, gain_one)
    grad_token_part, grad_gain_one = norm_back(grad_normed)
    grad_tokens = (grad_residual + grad_token_part)[None]
    in_rows = grad_in_part.shape[0] // fsdp
    in_own = scattered_sum(grad_in_part.reshape(fsdp, in_rows, D), "fsdp", fsdp_order)
    in_granules = in_own.astype(heads_low).reshape(in_rows // 64, 64, D)
    reduced_in = jnp.concatenate(routed(in_granules, in_targets(seq, fsdp), both, me))

    grad_projection = lax.dot_general(
        grad_small, normed_low.astype(jnp.float32), (((0,), (0,)), ((), ())), precision=PRECISE
    )
    width = 2 * DKH + DVH
    compact = jnp.concatenate(
        [
            grad_projection.reshape(-1),
            grad_taps.reshape(-1),
            grad_gain_one,
            grad_gain_two,
            grad_gain_head,
            grad_rate.reshape(1),
            grad_bias.reshape(1),
        ]
    )
    fill = -compact.shape[0] % 1024
    compact = jnp.concatenate([compact, jnp.zeros((fill,), jnp.float32)]).reshape(-1, 128)
    compact = summed_everywhere(compact, [("fsdp", bit) for bit in range(fsdp_bits)])
    compact = gathered(compact, "seq", list(range(seq_bits))).reshape(seq, -1)
    cuts = [2 * D, KCONV * width, D, D, DVH, 1, 1]
    places = [sum(cuts[:i]) for i in range(len(cuts))]
    take = lambda i: compact[:, places[i] : places[i] + cuts[i]]
    taps_all = take(1).reshape(seq, KCONV, width)
    spread_taps = lambda a, b: jnp.transpose(taps_all[:, :, a:b], (1, 0, 2)).reshape(KCONV, -1)
    grad_vector = jnp.concatenate(
        [
            jnp.transpose(take(0).reshape(seq, 2, D), (1, 0, 2)).reshape(-1),
            jnp.concatenate(
                [spread_taps(0, DKH), spread_taps(DKH, 2 * DKH), spread_taps(2 * DKH, width)],
                axis=1,
            ).reshape(-1),
            jnp.sum(take(2), axis=0),
            jnp.sum(take(3), axis=0),
            jnp.sum(take(4), axis=0),
            take(5).reshape(-1),
            take(6).reshape(-1),
        ]
    )

    squares = (
        jnp.sum(reduced_in * reduced_in)
        + jnp.sum(reduced_out * reduced_out)
        + jnp.sum(reduced_up * reduced_up)
        + jnp.sum(reduced_down * reduced_down)
    )
    all_bits = [("fsdp", bit) for bit in range(fsdp_bits)] + [("seq", bit) for bit in range(seq_bits)]
    squares = summed_everywhere(jnp.full((8, 128), squares), all_bits)[0, 0]
    grad_norm = jnp.sqrt(squares + jnp.sum(grad_vector * grad_vector))
    clipping = jnp.minimum(1.0, CLIP_NORM / (grad_norm + 1e-06))
    reduced = (reduced_in, reduced_out, reduced_up, reduced_down)
    momenta = (momentum_in, momentum_out, momentum_up, momentum_down)
    renewed = [MOMENTUM * m + (1.0 - MOMENTUM) * clipping * g for m, g in zip(momenta, reduced)]
    blocks = jnp.stack([block for one in renewed for block in gram_panels(one)])
    blocks = lax.psum(blocks.astype(heads_low), both)
    updates = [
        thin_update(one, gram_whole(blocks[10 * i : 10 * i + 10]), one.shape[0] * seq * fsdp)
        for i, one in enumerate(renewed)
    ]
    clipped = clipping * grad_vector
    first_next = ADAM_ONE * first_moment + (1.0 - ADAM_ONE) * clipped
    second_next = ADAM_TWO * second_moment + (1.0 - ADAM_TWO) * clipped * clipped
    update_vector = (
        -VECTOR_RATE
        * (first_next / (1.0 - ADAM_ONE**STEP))
        / (jnp.sqrt(second_next / (1.0 - ADAM_TWO**STEP)) + ADAM_EPS)
    )
    return (
        mixed,
        grad_tokens,
        *reduced,
        *renewed,
        *updates,
        grad_vector,
        first_next,
        second_next,
        update_vector,
        grad_norm.reshape(1),
    )


def fits_pairs(mesh, sequences):
    seq, fsdp = (mesh.shape["seq"], mesh.shape["fsdp"])
    return seq == H and fsdp == 4 and sequences == fsdp


def solution(mesh):
    in_specs = (
        P("fsdp", "seq", None),
        P("fsdp", "seq", None),
        P("fsdp", "seq"),
        P("fsdp", None),
        P("fsdp", None),
        P("fsdp", None),
        P("fsdp", None),
        P(),
        P(("seq", "fsdp"), None),
        P(("seq", "fsdp"), None),
        P(("seq", "fsdp"), None),
        P(("seq", "fsdp"), None),
        P(),
        P(),
    )
    out_specs = (
        P("fsdp", "seq", None),
        P("fsdp", "seq", None),
        P(("seq", "fsdp"), None),
        P(("seq", "fsdp"), None),
        P(("seq", "fsdp"), None),
        P(("seq", "fsdp"), None),
        P(("seq", "fsdp"), None),
        P(("seq", "fsdp"), None),
        P(("seq", "fsdp"), None),
        P(("seq", "fsdp"), None),
        P(("seq", "fsdp"), None),
        P(("seq", "fsdp"), None),
        P(("seq", "fsdp"), None),
        P(("seq", "fsdp"), None),
        P(),
        P(),
        P(),
        P(),
        P(),
    )

    def step(tokens, *rest):
        local = pair_shards if fits_pairs(mesh, tokens.shape[0]) else shards
        return jax.shard_map(
            local, mesh=mesh, in_specs=in_specs, out_specs=out_specs, check_vma=False
        )(tokens, *rest)

    return step
```

```python
import math

import jax
import jax.numpy as jnp
from jax import lax
from jax.experimental import pallas as pl
from jax.experimental.pallas import tpu as pltpu
from jax.sharding import PartitionSpec as P

D = 1024
H = 8
DKH = 128
DVH = 256
FF = 2816
KCONV = 4
STRETCH = 64
NS_ITERS = 2
STEP = 10


PRECISE = lax.Precision.HIGHEST
RMS_EPS = 1e-06
NS_A = 3.4445
NS_B = -4.775
NS_C = 2.0315
MOMENTUM = 0.95
ADAM_ONE = 0.9
ADAM_TWO = 0.95
LEARN_RATE = 0.02
VECTOR_RATE = 0.01
CLIP_NORM = 1.0
ADAM_EPS = 1e-08


def passed_along(value, axis, steps):
    count = lax.axis_size(axis)
    first, last = (max(0, -steps), min(count, count - steps))
    return lax.ppermute(value, axis, [(source, source + steps) for source in range(first, last)])


def entering(value, axis, join, neutral):
    count, mine = (lax.axis_size(axis), lax.axis_index(axis))
    pieces = jax.tree.map(lambda part: lax.all_gather(part, axis), value)
    running = jax.tree.map(
        lambda part, zero: jnp.full_like(part, 0) + jnp.asarray(zero, part.dtype), value, neutral
    )

    def entering_hop(position, running):
        longer = join(running, jax.tree.map(lambda part: part[position], pieces))
        return jax.tree.map(lambda new, old: jnp.where(position < mine, new, old), longer, running)

    return lax.fori_loop(0, count - 1, entering_hop, running)


def prefix_2(value, axis, combine, identity):
    count, index = (lax.axis_size(axis), lax.axis_index(axis))
    everything = jax.tree.map(
        lambda part, kind: lax.all_gather(part.astype(kind), axis),
        value,
        jax.tree.map(lambda a: jnp.bfloat16 if a.dtype == jnp.float32 else a.dtype, value),
    )
    start = jax.tree.map(
        lambda part, zero: jnp.broadcast_to(jnp.asarray(zero, part.dtype), part.shape),
        value,
        identity,
    )

    def prefix_hop(k, before):
        at = count - 1 - k
        reached = at > index
        new = combine(
            before, jax.tree.map(lambda part, own: part[at].astype(own.dtype), everything, value)
        )
        return jax.tree.map(lambda a, b: jnp.where(reached, a, b), new, before)

    return lax.fori_loop(0, count, prefix_hop, start)


def unpack_vectors(vectors):
    widths = [2 * H * D, KCONV * (2 * H * DKH + H * DVH), D, D, DVH, H, H]
    pieces = []
    offset = 0
    for span_width in widths:
        pieces.append(vectors[offset : offset + span_width])
        offset += span_width
    projection = pieces[0].reshape(2 * H, D)
    conv_taps = pieces[1].reshape(KCONV, 2 * H * DKH + H * DVH)
    return (projection, conv_taps, pieces[2], pieces[3], pieces[4], pieces[5], pieces[6])


def rms_scale(values, gain):
    inverse = lax.rsqrt(jnp.mean(values * values, axis=-1, keepdims=True) + RMS_EPS)
    return values * inverse * gain


def swiglu(values):
    return jax.nn.silu(values[:, :FF]) * values[:, FF:]


def contract_last(left, right):
    return lax.dot_general(
        left, right, (((1,), (1,)), ((), ())), preferred_element_type=jnp.float32
    )


def contract_first(left, right):
    return lax.dot_general(
        left, right, (((0,), (0,)), ((), ())), preferred_element_type=jnp.float32
    )


def short_conv(extended, extended_ids, tap_weights):
    out_rows = extended.shape[0] - (KCONV - 1)
    current_ids = extended_ids[KCONV - 1 :]
    summed = jnp.zeros((out_rows, extended.shape[1]), jnp.float32)
    for tap_index in range(KCONV):
        same_document = (extended_ids[tap_index : tap_index + out_rows] == current_ids).astype(
            jnp.float32
        )
        summed = (
            summed
            + tap_weights[tap_index]
            * extended[tap_index : tap_index + out_rows]
            * same_document[:, None]
        )
    return jax.nn.silu(summed)


def delta_block(carry_state, block_inputs):
    queries, keys_unit, values, beta_rates, log_decay, block_ids, before_id = block_inputs
    length_block = block_ids.shape[0]
    cumulative = jnp.cumsum(log_decay, axis=0).T
    row_index = lax.broadcasted_iota(jnp.int32, (length_block, length_block), 0)
    col_index = lax.broadcasted_iota(jnp.int32, (length_block, length_block), 1)
    linked = (row_index >= col_index) & (block_ids[:, None] == block_ids[None, :])
    spread = cumulative[:, :, None] - cumulative[:, None, :]
    ratios = jnp.where(linked[None], jnp.exp(jnp.where(linked[None], spread, 0.0)), 0.0)
    carried = jnp.exp(cumulative) * (block_ids == before_id).astype(jnp.float32)[None, :]
    beta_heads = beta_rates.T
    key_gram = jnp.einsum("thd,shd->hts", keys_unit, keys_unit, precision=PRECISE)
    cross_gram = jnp.einsum("thd,shd->hts", queries, keys_unit, precision=PRECISE)
    strict = jnp.where((row_index > col_index)[None], ratios * key_gram, 0.0)
    system = jnp.eye(length_block, dtype=jnp.float32)[None] + beta_heads[:, :, None] * strict
    key_state = jnp.einsum("thd,hdw->htw", keys_unit, carry_state, precision=PRECISE)
    value_heads = jnp.transpose(values, (1, 0, 2))
    target = beta_heads[:, :, None] * (value_heads - carried[:, :, None] * key_state)
    solved = jax.scipy.linalg.solve_triangular(system, target, lower=True, unit_diagonal=True)
    query_state = jnp.einsum("thd,hdw->htw", queries, carry_state, precision=PRECISE)
    outputs = carried[:, :, None] * query_state + jnp.einsum(
        "hts,hsw->htw", ratios * cross_gram, solved, precision=PRECISE
    )
    last_ratios = ratios[:, length_block - 1, :]
    new_state = carried[:, length_block - 1][:, None, None] * carry_state + jnp.einsum(
        "shd,hs,hsw->hdw", keys_unit, last_ratios, solved, precision=PRECISE
    )
    return (new_state, jnp.transpose(outputs, (1, 0, 2)))


def mixer_core(
    extended,
    extended_ids,
    normed_in,
    tap_weights,
    small_weights,
    decay_log,
    decay_bias,
    start_state,
    first_id,
):
    count_rows = normed_in.shape[0]
    conv_out = short_conv(extended, extended_ids, tap_weights)
    small = jnp.dot(normed_in, small_weights.T, precision=PRECISE)
    beta_rates = jax.nn.sigmoid(small[:, :H])
    log_decay = -jnp.exp(decay_log) * jax.nn.softplus(small[:, H:] + decay_bias)
    queries = conv_out[:, : H * DKH].reshape(count_rows, H, DKH)
    queries = (
        queries
        * lax.rsqrt(jnp.sum(queries * queries, axis=-1, keepdims=True) + RMS_EPS)
        * DKH ** (-0.5)
    )
    keys_unit = conv_out[:, H * DKH : 2 * H * DKH].reshape(count_rows, H, DKH)
    keys_unit = keys_unit * lax.rsqrt(
        jnp.sum(keys_unit * keys_unit, axis=-1, keepdims=True) + RMS_EPS
    )
    values = conv_out[:, 2 * H * DKH :].reshape(count_rows, H, DVH)
    extra_width = start_state.shape[2] - DVH
    values = jnp.concatenate([values, jnp.zeros((count_rows, H, extra_width), jnp.float32)], axis=2)
    blocks = count_rows // STRETCH
    row_ids = extended_ids[KCONV - 1 :].reshape(blocks, STRETCH)
    before_ids = jnp.concatenate([jnp.reshape(first_id, (1,)), row_ids[: blocks - 1, STRETCH - 1]])
    final_state, outputs = lax.scan(
        jax.checkpoint(delta_block),
        start_state,
        (
            queries.reshape(blocks, STRETCH, H, DKH),
            keys_unit.reshape(blocks, STRETCH, H, DKH),
            values.reshape(blocks, STRETCH, H, start_state.shape[2]),
            beta_rates.reshape(blocks, STRETCH, H),
            log_decay.reshape(blocks, STRETCH, H),
            row_ids,
            before_ids,
        ),
    )
    return (outputs.reshape(count_rows, H, start_state.shape[2]), final_state)


def compose_maps(earlier, later):
    return (
        jnp.einsum("hij,hjk->hik", later[0], earlier[0], precision=PRECISE),
        jnp.einsum("hij,hjw->hiw", later[0], earlier[1], precision=PRECISE) + later[1],
    )


def muon_update(block_rows, gram, total_rows):
    inverse_norm = 1.0 / (jnp.sqrt(jnp.trace(gram)) + 1e-07)
    current = gram * (inverse_norm * inverse_norm)
    identity = jnp.eye(gram.shape[0], dtype=jnp.float32)
    ortho = block_rows * inverse_norm
    for iteration in range(NS_ITERS):
        square = jnp.dot(current, current, precision=PRECISE)
        factor = NS_A * identity + NS_B * current + NS_C * square
        ortho = jnp.dot(ortho, factor, precision=PRECISE)
        if iteration + 1 < NS_ITERS:
            current = jnp.dot(
                current, jnp.dot(factor, factor, precision=PRECISE), precision=PRECISE
            )
    return -LEARN_RATE * 0.2 * math.sqrt(max(total_rows, D)) * ortho


def self_gram(matrix):
    return lax.dot_general(matrix, matrix, (((0,), (0,)), ((), ())), precision=PRECISE)


def shards(
    tokens,
    cotangent,
    segments,
    weight_in,
    weight_out,
    weight_up,
    weight_down,
    vectors,
    momentum_in,
    momentum_out,
    momentum_up,
    momentum_down,
    first_moment,
    second_moment,
):
    projection, conv_taps, gain_one, gain_two, gain_head, decay_log, decay_bias = unpack_vectors(
        vectors
    )
    full_in, full_out, full_up, full_down = (
        lax.all_gather(weight_in.astype(jnp.bfloat16), "fsdp", axis=0, tiled=True),
        lax.all_gather(weight_out.astype(jnp.bfloat16), "fsdp", axis=0, tiled=True),
        lax.all_gather(weight_up.astype(jnp.bfloat16), "fsdp", axis=0, tiled=True),
        lax.all_gather(weight_down.astype(jnp.bfloat16), "fsdp", axis=0, tiled=True),
    )
    token_rows = tokens[0].astype(jnp.float32)
    count_rows = token_rows.shape[0]
    conv_width = 2 * H * DKH + H * DVH
    id_plus = segments[0].astype(jnp.float32) + 1.0
    normed, norm_back = jax.vjp(rms_scale, token_rows, gain_one)
    normed_low = normed.astype(jnp.bfloat16)
    projected = contract_last(normed_low, full_in).astype(jnp.bfloat16)
    conv_low = projected[:, :conv_width]
    gate_low = projected[:, conv_width:]
    edge_rows, edge_ids = passed_along(
        (
            conv_low[count_rows - KCONV + 1 :],
            id_plus[count_rows - KCONV + 1 :].astype(jnp.bfloat16),
        ),
        "seq",
        1,
    )
    extended_ids = jnp.concatenate([edge_ids.astype(jnp.float32), id_plus])
    extended = jnp.concatenate([edge_rows, conv_low], axis=0).astype(jnp.float32)
    identity = jnp.broadcast_to(jnp.eye(DKH, dtype=jnp.float32), (H, DKH, DKH))
    zero_state = jnp.zeros((H, DKH, DVH), jnp.float32)
    start_state = jnp.concatenate([zero_state, identity], axis=2)

    def mixer_local(conv_values, normed_values, tap_weights, small_weights, rates, rate_bias):
        return mixer_core(
            conv_values,
            extended_ids,
            normed_values,
            tap_weights,
            small_weights,
            rates,
            rate_bias,
            start_state,
            extended_ids[KCONV - 2],
        )

    (local_out, final_state), mixer_back = jax.vjp(
        mixer_local,
        extended,
        normed_low.astype(jnp.float32),
        conv_taps,
        projection,
        decay_log,
        decay_bias,
    )
    own_part = local_out[:, :, :DVH]
    reach_rows = local_out[:, :, DVH:]
    carry_state = final_state[:, :, :DVH]
    transfer = final_state[:, :, DVH:]
    prefix = entering((transfer, carry_state), "seq", compose_maps, (identity, zero_state))
    state_in = prefix[1]
    recurrent = own_part + jnp.einsum("thi,hiw->thw", reach_rows, state_in, precision=PRECISE)

    def gate_local(recurrent_values, gate_values, head_gain):
        return rms_scale(recurrent_values, head_gain).reshape(count_rows, H * DVH) * jax.nn.silu(
            gate_values
        )

    gated, gate_back = jax.vjp(gate_local, recurrent, gate_low.astype(jnp.float32), gain_head)
    gated_low = gated.astype(jnp.bfloat16)
    attention = jnp.dot(gated_low, full_out, preferred_element_type=jnp.float32)
    residual = token_rows + attention
    normed_two, norm_two_back = jax.vjp(rms_scale, residual, gain_two)
    normed_two_low = normed_two.astype(jnp.bfloat16)
    gate_up = contract_last(normed_two_low, full_up)
    hidden, swiglu_back = jax.vjp(swiglu, gate_up)
    hidden_low = hidden.astype(jnp.bfloat16)
    feed_out = jnp.dot(hidden_low, full_down, preferred_element_type=jnp.float32)
    mixed = (residual + feed_out).astype(jnp.bfloat16)[None]
    back_in, back_out, back_up, back_down = (full_in, full_out, full_up, full_down)
    grad_rows = cotangent[0].astype(jnp.float32)
    grad_feed_low = cotangent[0]
    grad_down = contract_first(hidden_low, grad_feed_low)
    grad_hidden = contract_last(grad_feed_low, back_down)
    (grad_gate_up,) = swiglu_back(grad_hidden)
    grad_gate_up_low = grad_gate_up.astype(jnp.bfloat16)
    grad_up = contract_first(grad_gate_up_low, normed_two_low)
    grad_normed_two = jnp.dot(grad_gate_up_low, back_up, preferred_element_type=jnp.float32)
    grad_resid_part, grad_gain_two = norm_two_back(grad_normed_two)
    grad_residual = grad_rows + grad_resid_part
    grad_attn_low = grad_residual.astype(jnp.bfloat16)
    grad_wout = contract_first(gated_low, grad_attn_low)
    grad_gated = contract_last(grad_attn_low, back_out)
    grad_recurrent, grad_gate_in, grad_gain_head = gate_back(grad_gated)
    grad_state_local = jnp.einsum("thi,thw->hiw", reach_rows, grad_recurrent, precision=PRECISE)
    grad_reach = jnp.einsum("thw,hiw->thi", grad_recurrent, state_in, precision=PRECISE)
    back_prefix = prefix_2(
        (jnp.swapaxes(transfer, 1, 2), grad_state_local),
        "seq",
        compose_maps,
        (identity, zero_state),
    )
    grad_after = back_prefix[1]
    grad_transfer = jnp.einsum("hiw,hjw->hij", grad_after, state_in, precision=PRECISE)
    grad_outputs = jnp.concatenate([grad_recurrent, grad_reach], axis=2)
    grad_final = jnp.concatenate([grad_after, grad_transfer], axis=2)
    (
        grad_extended,
        grad_normed_small,
        grad_taps,
        grad_projection,
        grad_decay_log,
        grad_decay_bias,
    ) = mixer_back((grad_outputs, grad_final))
    from_next = passed_along(grad_extended[: KCONV - 1].astype(jnp.bfloat16), "seq", -1).astype(
        jnp.float32
    )
    grad_conv = grad_extended[KCONV - 1 :]
    grad_conv = jnp.concatenate(
        [grad_conv[: count_rows - KCONV + 1], grad_conv[count_rows - KCONV + 1 :] + from_next],
        axis=0,
    )
    grad_projected_low = jnp.concatenate([grad_conv, grad_gate_in], axis=1).astype(jnp.bfloat16)
    grad_win = contract_first(grad_projected_low, normed_low)
    grad_normed = (
        jnp.dot(grad_projected_low, back_in, preferred_element_type=jnp.float32) + grad_normed_small
    )
    grad_token_part, grad_gain_one = norm_back(grad_normed)
    grad_tokens = (grad_residual + grad_token_part)[None]
    reduced_in, reduced_out, reduced_up, reduced_down = (
        lax.psum_scatter(grad_win, ("seq", "fsdp"), scatter_dimension=0, tiled=True),
        lax.psum_scatter(grad_wout, ("seq", "fsdp"), scatter_dimension=0, tiled=True),
        lax.psum_scatter(grad_up, ("seq", "fsdp"), scatter_dimension=0, tiled=True),
        lax.psum_scatter(grad_down, ("seq", "fsdp"), scatter_dimension=0, tiled=True),
    )
    grad_vector_part = jnp.concatenate(
        [
            grad_projection.reshape(-1),
            grad_taps.reshape(-1),
            grad_gain_one,
            grad_gain_two,
            grad_gain_head,
            grad_decay_log,
            grad_decay_bias,
        ]
    )
    squares_local = (
        jnp.sum(reduced_in * reduced_in)
        + jnp.sum(reduced_out * reduced_out)
        + jnp.sum(reduced_up * reduced_up)
        + jnp.sum(reduced_down * reduced_down)
    )
    grad_vector, squares_total = lax.psum((grad_vector_part, squares_local), ("seq", "fsdp"))
    grad_norm = jnp.sqrt(squares_total + jnp.sum(grad_vector * grad_vector))
    clipping = jnp.minimum(1.0, CLIP_NORM / (grad_norm + 1e-06))
    renewed_in = MOMENTUM * momentum_in + (1.0 - MOMENTUM) * clipping * reduced_in
    renewed_out = MOMENTUM * momentum_out + (1.0 - MOMENTUM) * clipping * reduced_out
    renewed_up = MOMENTUM * momentum_up + (1.0 - MOMENTUM) * clipping * reduced_up
    renewed_down = MOMENTUM * momentum_down + (1.0 - MOMENTUM) * clipping * reduced_down
    gram_in, gram_out, gram_up, gram_down = lax.psum(
        (
            self_gram(renewed_in),
            self_gram(renewed_out),
            self_gram(renewed_up),
            self_gram(renewed_down),
        ),
        ("seq", "fsdp"),
    )
    devices_all = lax.axis_size(("seq", "fsdp"))
    update_in = muon_update(renewed_in, gram_in, renewed_in.shape[0] * devices_all)
    update_out = muon_update(renewed_out, gram_out, renewed_out.shape[0] * devices_all)
    update_up = muon_update(renewed_up, gram_up, renewed_up.shape[0] * devices_all)
    update_down = muon_update(renewed_down, gram_down, renewed_down.shape[0] * devices_all)
    clipped = clipping * grad_vector
    first_next = ADAM_ONE * first_moment + (1.0 - ADAM_ONE) * clipped
    second_next = ADAM_TWO * second_moment + (1.0 - ADAM_TWO) * clipped * clipped
    update_vector = (
        -VECTOR_RATE
        * (first_next / (1.0 - ADAM_ONE**STEP))
        / (jnp.sqrt(second_next / (1.0 - ADAM_TWO**STEP)) + ADAM_EPS)
    )
    return (
        mixed,
        grad_tokens,
        reduced_in,
        reduced_out,
        reduced_up,
        reduced_down,
        renewed_in,
        renewed_out,
        renewed_up,
        renewed_down,
        update_in,
        update_out,
        update_up,
        update_down,
        grad_vector,
        first_next,
        second_next,
        update_vector,
        grad_norm.reshape(1),
    )


Z_LINE = ("seq", (1, 2))
X_PAIR = ("seq", (0,))
Y_PAIR = ("fsdp", (1,))
CORES = ("fsdp", (0,))
SEQ_LAYOUT = (Z_LINE, X_PAIR)
FSDP_LAYOUT = (Y_PAIR, CORES)


def exchanged(value, group, offset):
    axis, bits = group
    mask = sum(1 << bit for i, bit in enumerate(bits) if (offset >> i) & 1)
    return lax.ppermute(value, axis, [(i, i ^ mask) for i in range(lax.axis_size(axis))])


def place_in(group):
    axis, bits = group
    mine = lax.axis_index(axis)
    return sum(((mine >> bit) & 1) << i for i, bit in enumerate(bits))


def picked(value, index, position=0):
    return lax.dynamic_index_in_dim(value, index, position, keepdims=False)


def scattered_sum(parts, layout, order, wire=jnp.bfloat16):
    sizes = tuple(2 ** len(bits) for _, bits in layout)
    held = parts.reshape(sizes + parts.shape[1:])
    left = list(layout)
    for group in order:
        position, place = (left.index(group), place_in(group))
        total = picked(held, place, position).astype(jnp.float32)
        for offset in range(1, 2 ** len(group[1])):
            gone = picked(held, place ^ offset, position).astype(wire)
            total = total + exchanged(gone, group, offset).astype(jnp.float32)
        held = total
        left.remove(group)
    return held


def gathered(value, layout, order):
    held = value
    done = []
    for group in order:
        count, place = (2 ** len(group[1]), place_in(group))
        pieces = [held] + [exchanged(held, group, offset) for offset in range(1, count)]
        rows = []
        for k in range(count):
            row = pieces[0]
            for offset in range(1, count):
                row = jnp.where((place ^ k) == offset, pieces[offset], row)
            rows.append(row)
        spot = sum(1 for other in done if layout.index(other) < layout.index(group))
        held = jnp.stack(rows, axis=spot)
        done.append(group)
    return held.reshape((-1,) + value.shape)


def summed_over(value, group_list):
    for group in group_list:
        others = [exchanged(value, group, offset) for offset in range(1, 2 ** len(group[1]))]
        value = sum(others, value)
    return value


def matchings(targets, slots, count):
    remaining = {src: [(dst, i) for i, (dst, _) in enumerate(targets[src])] for src in range(count)}
    rounds = []
    for _ in range(slots):
        owner = {}

        def seek(src, seen):
            for dst, i in remaining[src]:
                if dst in seen:
                    continue
                seen.add(dst)
                if dst not in owner or seek(owner[dst][0], seen):
                    owner[dst] = (src, i)
                    return True
            return False

        for src in range(count):
            assert seek(src, set())
        chosen = {}
        for dst, (src, i) in owner.items():
            chosen[src] = (dst, i)
        for src, (dst, i) in chosen.items():
            remaining[src].remove((dst, i))
        rounds.append(chosen)
    return rounds


def routed(granules, targets, axes, me):
    slots, count = (len(targets[0]), len(targets))
    pieces = []
    for chosen in matchings(targets, slots, count):
        sent = jnp.asarray([chosen[src][1] for src in range(count)], jnp.int32)
        landing = [0] * count
        for src, (dst, i) in chosen.items():
            landing[dst] = targets[src][i][1]
        piece = lax.ppermute(
            picked(granules, sent[me]), axes, [(src, chosen[src][0]) for src in range(count)]
        )
        pieces.append((piece, jnp.asarray(landing, jnp.int32)[me]))
    return [
        sum(
            jnp.where(place == slot, piece.astype(jnp.float32), 0.0)
            for piece, place in pieces
        )
        for slot in range(slots)
    ]


CHUNK = 128
MIX = lax.Precision.HIGH


def product(spec, left, right):
    return jnp.einsum(spec, left, right, precision=MIX, preferred_element_type=jnp.float32)


def unit_inverse(strict):
    size = strict.shape[-1]
    rows = lax.broadcasted_iota(jnp.int32, (size, size), 0)
    cols = lax.broadcasted_iota(jnp.int32, (size, size), 1)
    exact = lambda a, b: jnp.einsum("nij,njk->nik", a, b, precision=PRECISE)
    eye = (rows == cols).astype(jnp.float32)[None]
    base = -jnp.where((rows // 8 == cols // 8)[None], strict, 0.0)
    second = exact(base, base)
    fourth = exact(second, second)
    inverse = eye + base
    inverse = inverse + exact(inverse, second)
    inverse = inverse + exact(inverse, fourth)
    width = 8
    while width < size:
        joint = (rows // (2 * width) == cols // (2 * width)) & (rows // width != cols // width)
        inverse = inverse - exact(exact(inverse, jnp.where(joint[None], strict, 0.0)), inverse)
        width *= 2
    return inverse


@jax.custom_vjp
def solved_with(strict, right):
    return product("nij,njw->niw", unit_inverse(strict), right)


def solved_keep(strict, right):
    inverse = unit_inverse(strict)
    answer = product("nij,njw->niw", inverse, right)
    return answer, (inverse, answer)


def solved_back(kept, grad):
    inverse, answer = kept
    grad_right = product("nji,njw->niw", inverse, grad)
    return -product("niw,njw->nij", grad_right, answer), grad_right


solved_with.defvjp(solved_keep, solved_back)


def chunk_maps(queries, keys, values, beta, cumulative, linked, below, first_open):
    spread = cumulative[:, :, None] - cumulative[:, None, :]
    ratios = jnp.where(linked, jnp.exp(jnp.where(linked, spread, 0.0)), 0.0)
    carried = jnp.exp(cumulative) * first_open
    key_gram = product("ntd,nsd->nts", keys, keys)
    cross = ratios * product("ntd,nsd->nts", queries, keys)
    strict = beta[:, :, None] * jnp.where(below, ratios * key_gram, 0.0)
    right = beta[:, :, None] * jnp.concatenate([carried[:, :, None] * keys, values], axis=2)
    both = solved_with(strict, right)
    weighted = keys * ratios[:, -1, :, None]
    onward = product("nsd,nsw->ndw", weighted, both)
    outward = product("nts,nsw->ntw", cross, both)
    size = keys.shape[2]
    eye = jnp.eye(size, dtype=jnp.float32)[None]
    state_map = carried[:, -1][:, None, None] * eye - onward[:, :, :size]
    reach = carried[:, :, None] * queries - outward[:, :, :size]
    return state_map, onward[:, :, size:], reach, outward[:, :, size:]


def pair_inputs(conv_in, small, ids, taps, rate, bias):
    count = conv_in.shape[0]
    extended = jnp.concatenate([jnp.zeros((KCONV - 1, conv_in.shape[1]), jnp.float32), conv_in])
    extended_ids = jnp.concatenate([jnp.zeros((KCONV - 1,), jnp.float32), ids])
    conv_out = short_conv(extended, extended_ids, taps)
    beta = jax.nn.sigmoid(small[:, 0])
    log_decay = -jnp.exp(rate) * jax.nn.softplus(small[:, 1] + bias)
    queries = conv_out[:, :DKH]
    queries = (
        queries
        * lax.rsqrt(jnp.sum(queries * queries, axis=-1, keepdims=True) + RMS_EPS)
        * DKH ** (-0.5)
    )
    keys = conv_out[:, DKH : 2 * DKH]
    keys = keys * lax.rsqrt(jnp.sum(keys * keys, axis=-1, keepdims=True) + RMS_EPS)
    chunks = count // CHUNK
    cut = lambda a: a.reshape((chunks, CHUNK) + a.shape[1:])
    cumulative = jnp.cumsum(cut(log_decay), axis=1)
    return cut(queries), cut(keys), cut(conv_out[:, 2 * DKH :]), cut(beta), cumulative


def pair_masks(ids):
    chunks = ids.shape[0] // CHUNK
    cut = ids.reshape(chunks, CHUNK)
    rows = lax.broadcasted_iota(jnp.int32, (CHUNK, CHUNK), 0)
    cols = lax.broadcasted_iota(jnp.int32, (CHUNK, CHUNK), 1)
    linked = (rows >= cols)[None] & (cut[:, :, None] == cut[:, None, :])
    before = jnp.concatenate([jnp.zeros((1,), ids.dtype), cut[:-1, -1]])
    return linked, (rows > cols)[None], (cut == before[:, None]).astype(jnp.float32)


def states_forward(state_map, addend):
    state = jnp.zeros(addend.shape[1:], jnp.float32)
    entering_states = []
    for n in range(addend.shape[0]):
        entering_states.append(state)
        state = jnp.dot(state_map[n], state, precision=MIX) + addend[n]
    return jnp.stack(entering_states)


def states_backward(state_map, grad_entering):
    grad = jnp.zeros(grad_entering.shape[1:], jnp.float32)
    after = []
    for n in reversed(range(grad_entering.shape[0])):
        after.append(grad)
        grad = grad_entering[n] + jnp.einsum("ij,iw->jw", state_map[n], grad, precision=MIX)
    return jnp.stack(after[::-1])


BLOCK = 128
SIDE = D // BLOCK
PACK = SIDE * (SIDE + 1) // 2


def gram_kernel(rows_ref, blocks_ref):
    count = 0
    for i in range(SIDE):
        left = rows_ref[0, :, i * BLOCK : (i + 1) * BLOCK]
        panel = contract_first(left, rows_ref[0, :, i * BLOCK :])
        for j in range(SIDE - i):
            blocks_ref[count] = panel[:, j * BLOCK : (j + 1) * BLOCK].astype(jnp.bfloat16)
            count += 1


def gram_blocks(rows):
    count, height, width = rows.shape
    return pl.pallas_call(
        gram_kernel,
        grid=(count,),
        in_specs=[pl.BlockSpec((1, height, width), lambda m: (m, 0, 0))],
        out_specs=pl.BlockSpec((PACK, BLOCK, BLOCK), lambda m: (m, 0, 0)),
        out_shape=jax.ShapeDtypeStruct((count * PACK, BLOCK, BLOCK), jnp.bfloat16),
        name="gram_blocks",
    )(rows)


def muon_kernel(rates_ref, rows_ref, blocks_ref, out_ref, gram_ref):
    count = 0
    trace = jnp.zeros((BLOCK, BLOCK), jnp.float32)
    line = lax.broadcasted_iota(jnp.int32, (BLOCK, BLOCK), 0)
    column = lax.broadcasted_iota(jnp.int32, (BLOCK, BLOCK), 1)
    for i in range(SIDE):
        for j in range(i, SIDE):
            block = blocks_ref[count]
            gram_ref[i * BLOCK : (i + 1) * BLOCK, j * BLOCK : (j + 1) * BLOCK] = block
            if i == j:
                trace = trace + jnp.where(line == column, block.astype(jnp.float32), 0.0)
            else:
                turned = block.astype(jnp.float32).T.astype(jnp.bfloat16)
                gram_ref[j * BLOCK : (j + 1) * BLOCK, i * BLOCK : (i + 1) * BLOCK] = turned
            count += 1
    total = jnp.sum(jnp.sum(trace, axis=1, keepdims=True), axis=0, keepdims=True)
    inverse_norm = 1.0 / (jnp.sqrt(total) + 1e-07)
    squared = inverse_norm * inverse_norm

    def times(rows):
        narrow = rows.astype(jnp.bfloat16)
        return jnp.dot(narrow, gram_ref[...], preferred_element_type=jnp.float32) * squared

    def through(rows):
        once = times(rows)
        return NS_A * rows + NS_B * once + NS_C * times(once)

    def advanced(rows):
        return through(through(times(rows)))

    first = through(rows_ref[0] * inverse_norm)
    once = advanced(first)
    ortho = NS_A * first + NS_B * once + NS_C * advanced(once)
    out_ref[0] = ortho * rates_ref[pl.program_id(0)]


def muon_rows(rows, blocks, rates):
    count, height, width = rows.shape
    return pl.pallas_call(
        muon_kernel,
        grid_spec=pltpu.PrefetchScalarGridSpec(
            num_scalar_prefetch=1,
            grid=(count,),
            in_specs=[
                pl.BlockSpec((1, height, width), lambda m, _: (m, 0, 0)),
                pl.BlockSpec((PACK, BLOCK, BLOCK), lambda m, _: (m, 0, 0)),
            ],
            out_specs=pl.BlockSpec((1, height, width), lambda m, _: (m, 0, 0)),
            scratch_shapes=[pltpu.VMEM((D, D), jnp.bfloat16)],
        ),
        out_shape=jax.ShapeDtypeStruct(rows.shape, jnp.float32),
        name="muon_rows",
    )(rates, rows, blocks)


def blocks_everywhere(blocks):
    whole = blocks.reshape(2, 32, -1, BLOCK)
    halves = []
    for half, order in ((0, (CORES, Y_PAIR, X_PAIR, Z_LINE)), (1, (CORES, X_PAIR, Y_PAIR, Z_LINE))):
        own = scattered_sum(whole[half], order, order).astype(jnp.bfloat16)
        halves.append(gathered(own, order, order[::-1]))
    return jnp.stack(halves).reshape(blocks.shape)


def head_tables(fsdp):
    per = (2 * H * DKH + 2 * H * DVH) // fsdp // DKH
    give, find = ([], [])
    for head in range(H):
        wanted = [head, H + head] + [
            2 * H + base + 2 * head + k for base in (0, 2 * H) for k in range(2)
        ]
        lists = [[g % per for g in wanted if g // per == f] for f in range(fsdp)]
        seen = [0] * fsdp
        where = []
        for g in wanted:
            f = g // per
            where.append((f, seen[f]))
            seen[f] += 1
        most = 2
        assert max(len(one) for one in lists) <= most
        give.append([one + [0] * (most - len(one)) for one in lists])
        find.append([f * most + j for f, j in where])
    return give, find


def in_targets(seq, fsdp):
    granule = 64
    per = (2 * H * DKH + 2 * H * DVH) // (seq * fsdp) // granule
    targets = []
    for s in range(seq):
        rows = []
        for start, size in (
            (s * DKH, DKH),
            (H * DKH + s * DKH, DKH),
            (2 * H * DKH + s * DVH, DVH),
            (2 * H * DKH + H * DVH + s * DVH, DVH),
        ):
            rows += [start // granule + k for k in range(size // granule)]
        for f in range(fsdp):
            own = rows[f * per : (f + 1) * per]
            targets.append([(g // per, g % per) for g in own])
    return targets


def up_targets(seq, fsdp):
    piece = FF // (seq * fsdp)
    return [
        [((f * seq + s) // 2, (f * seq + s) % 2), (seq * fsdp // 2 + (f * seq + s) // 2, (f * seq + s) % 2)]
        for s in range(seq)
        for f in range(fsdp)
    ]


def block_targets(seq, fsdp):
    return [[(f * seq + s, 0)] for s in range(seq) for f in range(fsdp)]


def up_shuffle_targets(fsdp):
    half = fsdp // 2
    return [[(2 * (f % half) + k, f // half) for k in range(2)] for f in range(fsdp)]


def pair_shards(
    tokens,
    cotangent,
    segments,
    weight_in,
    weight_out,
    weight_up,
    weight_down,
    vectors,
    momentum_in,
    momentum_out,
    momentum_up,
    momentum_down,
    first_moment,
    second_moment,
):
    seq, fsdp = (lax.axis_size("seq"), lax.axis_size("fsdp"))
    head, group = (lax.axis_index("seq"), lax.axis_index("fsdp"))
    me = head * fsdp + group
    inward, outward = ((CORES, Y_PAIR), (Y_PAIR, CORES))
    projection, conv_taps, gain_one, gain_two, gain_head, decay_log, decay_bias = unpack_vectors(
        vectors
    )
    own = tokens.shape[1]
    length = own * seq
    heads_low = jnp.bfloat16

    row_ids = jnp.zeros((16, D), heads_low)
    row_ids = row_ids.at[0, :own].set((segments[0] + 1).astype(heads_low))
    packed = lax.all_gather(jnp.concatenate([tokens[0], row_ids]), "seq")

    give, find = head_tables(fsdp)
    give_table = jnp.asarray(give, jnp.int32)
    find_table = jnp.asarray(find, jnp.int32)
    slices = [
        lax.dynamic_slice_in_dim(weight_in, give_table[head, group, j] * DKH, DKH, 0)
        for j in range(2)
    ]
    given = gathered(jnp.stack(slices).astype(heads_low), FSDP_LAYOUT, outward)
    given = given.reshape(2 * fsdp, DKH, D)
    small_rows = jnp.stack([picked(projection, head), picked(projection, H + head)])
    taps_rows = conv_taps.reshape(KCONV, 4 * H, DKH)
    taps_head = jnp.concatenate(
        [
            picked(taps_rows, head, 1),
            picked(taps_rows, H + head, 1),
            picked(taps_rows, 2 * H + 2 * head, 1),
            picked(taps_rows, 2 * H + 2 * head + 1, 1),
        ],
        axis=1,
    )
    rate, bias = (decay_log[head], decay_bias[head])

    full_out = lax.all_gather(weight_out.astype(heads_low), "fsdp", axis=0, tiled=True)
    cot_group = gathered(cotangent[0], FSDP_LAYOUT, outward).reshape(fsdp * own, D)
    half_up = weight_up.shape[0] // 2
    up_gate, up_value = [
        part.astype(heads_low)
        for part in routed(
            weight_up.astype(heads_low).reshape(2, half_up, D), up_shuffle_targets(fsdp), "fsdp", group
        )
    ]
    packed, up_gate, up_value, given = lax.optimization_barrier((packed, up_gate, up_value, given))
    low_up = jnp.concatenate([up_gate, up_value])
    token_seq = packed[:, :own].reshape(length, D)
    ids = packed[:, own, :own].reshape(length).astype(jnp.float32)
    head_rows = jnp.concatenate([picked(given, find_table[head, j]) for j in range(6)])
    low_down = weight_down.astype(heads_low)

    token_rows = token_seq.astype(jnp.float32)
    scaled_rows = token_rows * lax.rsqrt(
        jnp.mean(token_rows * token_rows, axis=-1, keepdims=True) + RMS_EPS
    )
    normed_low = (scaled_rows * gain_one).astype(heads_low)
    projected = contract_last(normed_low, head_rows).astype(heads_low)
    conv_in = projected[:, : 2 * DKH + DVH].astype(jnp.float32)
    gate_in = projected[:, 2 * DKH + DVH :].astype(jnp.float32)
    small = lax.dot_general(
        normed_low.astype(jnp.float32), small_rows, (((1,), (1,)), ((), ())), precision=PRECISE
    )
    linked, below, first_open = pair_masks(ids)
    parts, inputs_back = jax.vjp(
        lambda c, m, t, r, b: pair_inputs(c, m, ids, t, r, b),
        conv_in,
        small,
        taps_head,
        rate,
        bias,
    )
    maps, maps_back = jax.vjp(
        lambda q, k, v, b, c: chunk_maps(q, k, v, b, c, linked, below, first_open), *parts
    )
    state_map, addend, reach, local = maps
    states = states_forward(state_map, addend)
    recurrent = (product("ntd,ndw->ntw", reach, states) + local).reshape(length, DVH)

    def gate_pair(recurrent_values, gate_values, head_gain):
        return rms_scale(recurrent_values, head_gain) * jax.nn.silu(gate_values)

    gated, gate_back = jax.vjp(gate_pair, recurrent, gate_in, gain_head)
    gated_low, cot_group = lax.optimization_barrier((gated.astype(heads_low), cot_group))
    gated_own = lax.all_to_all(gated_low.reshape(seq, own, DVH), "seq", 0, 0)
    gated_own = jnp.transpose(gated_own, (1, 0, 2)).reshape(own, H * DVH)

    own_rows = tokens[0].astype(jnp.float32)
    residual = own_rows + jnp.dot(gated_own, full_out, preferred_element_type=jnp.float32)
    normed_two, norm_two_back = jax.vjp(rms_scale, residual, gain_two)
    two_group = gathered(normed_two.astype(heads_low), FSDP_LAYOUT, outward)
    two_group = two_group.reshape(fsdp * own, D)
    gate_up = contract_last(two_group, low_up)
    units = half_up

    def swiglu_own(values):
        return jax.nn.silu(values[:, :units]) * values[:, units:]

    hidden, swiglu_back = jax.vjp(swiglu_own, gate_up)
    hidden_low = hidden.astype(heads_low)
    feed_parts = jnp.dot(hidden_low, low_down, preferred_element_type=jnp.float32)
    feed_out = scattered_sum(feed_parts.reshape(fsdp, own, D), FSDP_LAYOUT, inward)
    mixed = (residual + feed_out).astype(heads_low)[None]

    grad_hidden = contract_last(cot_group, low_down)
    (grad_gate_up,) = swiglu_back(grad_hidden)
    grad_gate_up_low = grad_gate_up.astype(heads_low)
    two_parts = jnp.dot(grad_gate_up_low, low_up, preferred_element_type=jnp.float32)
    grad_normed_two = scattered_sum(two_parts.reshape(fsdp, own, D), FSDP_LAYOUT, inward)
    grad_resid_part, grad_gain_two = norm_two_back(grad_normed_two)
    grad_residual = cotangent[0].astype(jnp.float32) + grad_resid_part
    grad_attn_low = grad_residual.astype(heads_low)
    grad_gated_own = contract_last(grad_attn_low, full_out).astype(heads_low)
    grad_gated_own = jnp.transpose(grad_gated_own.reshape(own, seq, DVH), (1, 0, 2))
    grad_gated = lax.all_to_all(grad_gated_own, "seq", 0, 0).reshape(length, DVH)

    grad_gated, grad_gate_up_late = lax.optimization_barrier((grad_gated, grad_gate_up_low))
    grad_down_part = contract_first(hidden_low, cot_group)
    grad_up_part = contract_first(grad_gate_up_late, two_group)
    gated_group = lax.all_to_all(gated_own.reshape(own, fsdp, -1), "fsdp", 1, 0)
    attn_group = gathered(grad_attn_low, FSDP_LAYOUT, outward).reshape(fsdp * own, D)
    grad_out_part = contract_first(gated_group.reshape(fsdp * own, -1), attn_group)
    piece, out_piece = (FF // (seq * fsdp), H * DVH // (seq * fsdp))
    late_parts = jnp.concatenate(
        [
            grad_down_part.astype(heads_low).reshape(seq, piece, D),
            grad_out_part.astype(heads_low).reshape(seq, out_piece, D),
            grad_up_part[: half_up].astype(heads_low).reshape(seq, piece, D),
            grad_up_part[half_up :].astype(heads_low).reshape(seq, piece, D),
        ],
        axis=1,
    )
    late_left = scattered_sum(late_parts[..., : D // 2], SEQ_LAYOUT, (X_PAIR, Z_LINE))
    late_right = scattered_sum(late_parts[..., D // 2 :], SEQ_LAYOUT, (Z_LINE, X_PAIR))
    late_own = jnp.concatenate([late_left, late_right], axis=-1).astype(heads_low)
    both = ("seq", "fsdp")
    (reduced_block,) = routed(
        late_own[None, : piece + out_piece], block_targets(seq, fsdp), both, me
    )
    reduced_down, reduced_out = (reduced_block[:piece], reduced_block[piece:])
    reduced_up = jnp.concatenate(
        routed(late_own[piece + out_piece :].reshape(2, piece, D), up_targets(seq, fsdp), both, me)
    )

    grad_gated = grad_gated.astype(jnp.float32)
    grad_recurrent, grad_gate_in, grad_gain_head = gate_back(grad_gated)
    grad_out_chunks = grad_recurrent.reshape(local.shape)
    grad_entering = product("ntd,ntw->ndw", reach, grad_out_chunks)
    grad_after = states_backward(state_map, grad_entering)
    grad_maps = (
        product("niw,njw->nij", grad_after, states),
        grad_after,
        product("ntw,ndw->ntd", grad_out_chunks, states),
        grad_out_chunks,
    )
    grad_conv, grad_small, grad_taps, grad_rate, grad_bias = inputs_back(maps_back(grad_maps))
    grad_projected_low = jnp.concatenate([grad_conv, grad_gate_in], axis=1).astype(heads_low)
    grad_in_part = contract_first(grad_projected_low, normed_low)
    normed_parts = jnp.dot(grad_projected_low, head_rows, preferred_element_type=jnp.float32)
    normed_parts = normed_parts + jnp.dot(grad_small, small_rows, precision=PRECISE)
    normed_low_parts = normed_parts.astype(heads_low).reshape(seq, own, D)
    normed_left = scattered_sum(normed_low_parts[..., : D // 2], SEQ_LAYOUT, (X_PAIR, Z_LINE))
    normed_right = scattered_sum(normed_low_parts[..., D // 2 :], SEQ_LAYOUT, (Z_LINE, X_PAIR))
    grad_normed = jnp.concatenate([normed_left, normed_right], axis=-1)
    _, norm_back = jax.vjp(rms_scale, own_rows, gain_one)
    grad_token_part, _ = norm_back(grad_normed)
    grad_gain_one = jnp.sum(normed_parts * scaled_rows, axis=0)
    grad_tokens = (grad_residual + grad_token_part)[None]
    in_rows = grad_in_part.shape[0] // fsdp
    in_own = scattered_sum(grad_in_part.reshape(fsdp, in_rows, D), FSDP_LAYOUT, inward)
    in_own = in_own.astype(heads_low)
    in_granules = in_own.reshape(in_rows // 64, 64, D)
    reduced_in = jnp.concatenate(routed(in_granules, in_targets(seq, fsdp), both, me))

    grad_projection = lax.dot_general(
        grad_small, normed_low.astype(jnp.float32), (((0,), (0,)), ((), ())), precision=PRECISE
    )
    width = 2 * DKH + DVH
    square = lambda part: jnp.sum(jnp.square(part.astype(jnp.float32)))
    compact = jnp.concatenate(
        [
            grad_projection.reshape(-1),
            grad_taps.reshape(-1),
            grad_gain_one,
            grad_gain_two,
            grad_gain_head,
            grad_rate.reshape(1),
            grad_bias.reshape(1),
            (square(in_own) + square(late_own)).reshape(1),
        ]
    )
    fill = -compact.shape[0] % 1024
    compact = jnp.concatenate([compact, jnp.zeros((fill,), jnp.float32)]).reshape(-1, 128)
    compact = summed_over(compact, [("fsdp", (0, 1))])
    compact = gathered(compact, SEQ_LAYOUT, (X_PAIR, Z_LINE)).reshape(seq, -1)
    cuts = [2 * D, KCONV * width, D, D, DVH, 1, 1, 1]
    places = [sum(cuts[:i]) for i in range(len(cuts))]
    take = lambda i: compact[:, places[i] : places[i] + cuts[i]]
    taps_all = take(1).reshape(seq, KCONV, width)
    spread_taps = lambda a, b: jnp.transpose(taps_all[:, :, a:b], (1, 0, 2)).reshape(KCONV, -1)
    grad_vector = jnp.concatenate(
        [
            jnp.transpose(take(0).reshape(seq, 2, D), (1, 0, 2)).reshape(-1),
            jnp.concatenate(
                [spread_taps(0, DKH), spread_taps(DKH, 2 * DKH), spread_taps(2 * DKH, width)],
                axis=1,
            ).reshape(-1),
            jnp.sum(take(2), axis=0),
            jnp.sum(take(3), axis=0),
            jnp.sum(take(4), axis=0),
            take(5).reshape(-1),
            take(6).reshape(-1),
        ]
    )

    squares = jnp.sum(take(7))
    grad_norm = jnp.sqrt(squares + jnp.sum(grad_vector * grad_vector))
    clipping = jnp.minimum(1.0, CLIP_NORM / (grad_norm + 1e-06))
    reduced = (reduced_in, reduced_out, reduced_up, reduced_down)
    momenta = (momentum_in, momentum_out, momentum_up, momentum_down)
    renewed = [MOMENTUM * m + (1.0 - MOMENTUM) * clipping * g for m, g in zip(momenta, reduced)]
    height = max(one.shape[0] for one in renewed)
    stacked = jnp.stack([jnp.pad(one, ((0, height - one.shape[0]), (0, 0))) for one in renewed])
    blocks = blocks_everywhere(gram_blocks(stacked.astype(heads_low)))
    rates = jnp.asarray(
        [-LEARN_RATE * 0.2 * math.sqrt(max(one.shape[0] * seq * fsdp, D)) for one in renewed],
        jnp.float32,
    )
    stacked = muon_rows(stacked, blocks, rates)
    updates = [stacked[i, : one.shape[0]] for i, one in enumerate(renewed)]
    clipped = clipping * grad_vector
    first_next = ADAM_ONE * first_moment + (1.0 - ADAM_ONE) * clipped
    second_next = ADAM_TWO * second_moment + (1.0 - ADAM_TWO) * clipped * clipped
    update_vector = (
        -VECTOR_RATE
        * (first_next / (1.0 - ADAM_ONE**STEP))
        / (jnp.sqrt(second_next / (1.0 - ADAM_TWO**STEP)) + ADAM_EPS)
    )
    return (
        mixed,
        grad_tokens,
        *reduced,
        *renewed,
        *updates,
        grad_vector,
        first_next,
        second_next,
        update_vector,
        grad_norm.reshape(1),
    )


def fits_pairs(mesh, sequences):
    seq, fsdp = (mesh.shape["seq"], mesh.shape["fsdp"])
    return seq == H and fsdp == 4 and sequences == fsdp


def solution(mesh):
    in_specs = (
        P("fsdp", "seq", None),
        P("fsdp", "seq", None),
        P("fsdp", "seq"),
        P("fsdp", None),
        P("fsdp", None),
        P("fsdp", None),
        P("fsdp", None),
        P(),
        P(("seq", "fsdp"), None),
        P(("seq", "fsdp"), None),
        P(("seq", "fsdp"), None),
        P(("seq", "fsdp"), None),
        P(),
        P(),
    )
    out_specs = (
        P("fsdp", "seq", None),
        P("fsdp", "seq", None),
        P(("seq", "fsdp"), None),
        P(("seq", "fsdp"), None),
        P(("seq", "fsdp"), None),
        P(("seq", "fsdp"), None),
        P(("seq", "fsdp"), None),
        P(("seq", "fsdp"), None),
        P(("seq", "fsdp"), None),
        P(("seq", "fsdp"), None),
        P(("seq", "fsdp"), None),
        P(("seq", "fsdp"), None),
        P(("seq", "fsdp"), None),
        P(("seq", "fsdp"), None),
        P(),
        P(),
        P(),
        P(),
        P(),
    )

    def step(tokens, *rest):
        local = pair_shards if fits_pairs(mesh, tokens.shape[0]) else shards
        return jax.shard_map(
            local, mesh=mesh, in_specs=in_specs, out_specs=out_specs, check_vma=False
        )(tokens, *rest)

    return step
```

```python
import math
from functools import partial

import jax
import jax.numpy as jnp
from jax import lax
from jax.experimental import pallas as pl
from jax.experimental.pallas import tpu as pltpu
from jax.sharding import PartitionSpec as P

D = 1024
H = 8
DKH = 128
DVH = 256
FF = 2816
KCONV = 4
STRETCH = 64
NS_ITERS = 2
STEP = 10


PRECISE = lax.Precision.HIGHEST
RMS_EPS = 1e-06
NS_A = 3.4445
NS_B = -4.775
NS_C = 2.0315
MOMENTUM = 0.95
ADAM_ONE = 0.9
ADAM_TWO = 0.95
LEARN_RATE = 0.02
VECTOR_RATE = 0.01
CLIP_NORM = 1.0
ADAM_EPS = 1e-08


def passed_along(value, axis, steps):
    count = lax.axis_size(axis)
    first, last = (max(0, -steps), min(count, count - steps))
    return lax.ppermute(value, axis, [(source, source + steps) for source in range(first, last)])


def entering(value, axis, join, neutral):
    count, mine = (lax.axis_size(axis), lax.axis_index(axis))
    pieces = jax.tree.map(lambda part: lax.all_gather(part, axis), value)
    running = jax.tree.map(
        lambda part, zero: jnp.full_like(part, 0) + jnp.asarray(zero, part.dtype), value, neutral
    )

    def entering_hop(position, running):
        longer = join(running, jax.tree.map(lambda part: part[position], pieces))
        return jax.tree.map(lambda new, old: jnp.where(position < mine, new, old), longer, running)

    return lax.fori_loop(0, count - 1, entering_hop, running)


def prefix_2(value, axis, combine, identity):
    count, index = (lax.axis_size(axis), lax.axis_index(axis))
    everything = jax.tree.map(
        lambda part, kind: lax.all_gather(part.astype(kind), axis),
        value,
        jax.tree.map(lambda a: jnp.bfloat16 if a.dtype == jnp.float32 else a.dtype, value),
    )
    start = jax.tree.map(
        lambda part, zero: jnp.broadcast_to(jnp.asarray(zero, part.dtype), part.shape),
        value,
        identity,
    )

    def prefix_hop(k, before):
        at = count - 1 - k
        reached = at > index
        new = combine(
            before, jax.tree.map(lambda part, own: part[at].astype(own.dtype), everything, value)
        )
        return jax.tree.map(lambda a, b: jnp.where(reached, a, b), new, before)

    return lax.fori_loop(0, count, prefix_hop, start)


def unpack_vectors(vectors):
    widths = [2 * H * D, KCONV * (2 * H * DKH + H * DVH), D, D, DVH, H, H]
    pieces = []
    offset = 0
    for span_width in widths:
        pieces.append(vectors[offset : offset + span_width])
        offset += span_width
    projection = pieces[0].reshape(2 * H, D)
    conv_taps = pieces[1].reshape(KCONV, 2 * H * DKH + H * DVH)
    return (projection, conv_taps, pieces[2], pieces[3], pieces[4], pieces[5], pieces[6])


def rms_scale(values, gain):
    inverse = lax.rsqrt(jnp.mean(values * values, axis=-1, keepdims=True) + RMS_EPS)
    return values * inverse * gain


def swiglu(values):
    return jax.nn.silu(values[:, :FF]) * values[:, FF:]


def contract_last(left, right):
    return lax.dot_general(
        left, right, (((1,), (1,)), ((), ())), preferred_element_type=jnp.float32
    )


def contract_first(left, right):
    return lax.dot_general(
        left, right, (((0,), (0,)), ((), ())), preferred_element_type=jnp.float32
    )


def short_conv(extended, extended_ids, tap_weights):
    out_rows = extended.shape[0] - (KCONV - 1)
    current_ids = extended_ids[KCONV - 1 :]
    summed = jnp.zeros((out_rows, extended.shape[1]), jnp.float32)
    for tap_index in range(KCONV):
        same_document = (extended_ids[tap_index : tap_index + out_rows] == current_ids).astype(
            jnp.float32
        )
        summed = (
            summed
            + tap_weights[tap_index]
            * extended[tap_index : tap_index + out_rows]
            * same_document[:, None]
        )
    return jax.nn.silu(summed)


def delta_block(carry_state, block_inputs):
    queries, keys_unit, values, beta_rates, log_decay, block_ids, before_id = block_inputs
    length_block = block_ids.shape[0]
    cumulative = jnp.cumsum(log_decay, axis=0).T
    row_index = lax.broadcasted_iota(jnp.int32, (length_block, length_block), 0)
    col_index = lax.broadcasted_iota(jnp.int32, (length_block, length_block), 1)
    linked = (row_index >= col_index) & (block_ids[:, None] == block_ids[None, :])
    spread = cumulative[:, :, None] - cumulative[:, None, :]
    ratios = jnp.where(linked[None], jnp.exp(jnp.where(linked[None], spread, 0.0)), 0.0)
    carried = jnp.exp(cumulative) * (block_ids == before_id).astype(jnp.float32)[None, :]
    beta_heads = beta_rates.T
    key_gram = jnp.einsum("thd,shd->hts", keys_unit, keys_unit, precision=PRECISE)
    cross_gram = jnp.einsum("thd,shd->hts", queries, keys_unit, precision=PRECISE)
    strict = jnp.where((row_index > col_index)[None], ratios * key_gram, 0.0)
    system = jnp.eye(length_block, dtype=jnp.float32)[None] + beta_heads[:, :, None] * strict
    key_state = jnp.einsum("thd,hdw->htw", keys_unit, carry_state, precision=PRECISE)
    value_heads = jnp.transpose(values, (1, 0, 2))
    target = beta_heads[:, :, None] * (value_heads - carried[:, :, None] * key_state)
    solved = jax.scipy.linalg.solve_triangular(system, target, lower=True, unit_diagonal=True)
    query_state = jnp.einsum("thd,hdw->htw", queries, carry_state, precision=PRECISE)
    outputs = carried[:, :, None] * query_state + jnp.einsum(
        "hts,hsw->htw", ratios * cross_gram, solved, precision=PRECISE
    )
    last_ratios = ratios[:, length_block - 1, :]
    new_state = carried[:, length_block - 1][:, None, None] * carry_state + jnp.einsum(
        "shd,hs,hsw->hdw", keys_unit, last_ratios, solved, precision=PRECISE
    )
    return (new_state, jnp.transpose(outputs, (1, 0, 2)))


def mixer_core(
    extended,
    extended_ids,
    normed_in,
    tap_weights,
    small_weights,
    decay_log,
    decay_bias,
    start_state,
    first_id,
):
    count_rows = normed_in.shape[0]
    conv_out = short_conv(extended, extended_ids, tap_weights)
    small = jnp.dot(normed_in, small_weights.T, precision=PRECISE)
    beta_rates = jax.nn.sigmoid(small[:, :H])
    log_decay = -jnp.exp(decay_log) * jax.nn.softplus(small[:, H:] + decay_bias)
    queries = conv_out[:, : H * DKH].reshape(count_rows, H, DKH)
    queries = (
        queries
        * lax.rsqrt(jnp.sum(queries * queries, axis=-1, keepdims=True) + RMS_EPS)
        * DKH ** (-0.5)
    )
    keys_unit = conv_out[:, H * DKH : 2 * H * DKH].reshape(count_rows, H, DKH)
    keys_unit = keys_unit * lax.rsqrt(
        jnp.sum(keys_unit * keys_unit, axis=-1, keepdims=True) + RMS_EPS
    )
    values = conv_out[:, 2 * H * DKH :].reshape(count_rows, H, DVH)
    extra_width = start_state.shape[2] - DVH
    values = jnp.concatenate([values, jnp.zeros((count_rows, H, extra_width), jnp.float32)], axis=2)
    blocks = count_rows // STRETCH
    row_ids = extended_ids[KCONV - 1 :].reshape(blocks, STRETCH)
    before_ids = jnp.concatenate([jnp.reshape(first_id, (1,)), row_ids[: blocks - 1, STRETCH - 1]])
    final_state, outputs = lax.scan(
        jax.checkpoint(delta_block),
        start_state,
        (
            queries.reshape(blocks, STRETCH, H, DKH),
            keys_unit.reshape(blocks, STRETCH, H, DKH),
            values.reshape(blocks, STRETCH, H, start_state.shape[2]),
            beta_rates.reshape(blocks, STRETCH, H),
            log_decay.reshape(blocks, STRETCH, H),
            row_ids,
            before_ids,
        ),
    )
    return (outputs.reshape(count_rows, H, start_state.shape[2]), final_state)


def compose_maps(earlier, later):
    return (
        jnp.einsum("hij,hjk->hik", later[0], earlier[0], precision=PRECISE),
        jnp.einsum("hij,hjw->hiw", later[0], earlier[1], precision=PRECISE) + later[1],
    )


def muon_update(block_rows, gram, total_rows):
    inverse_norm = 1.0 / (jnp.sqrt(jnp.trace(gram)) + 1e-07)
    current = gram * (inverse_norm * inverse_norm)
    identity = jnp.eye(gram.shape[0], dtype=jnp.float32)
    ortho = block_rows * inverse_norm
    for iteration in range(NS_ITERS):
        square = jnp.dot(current, current, precision=PRECISE)
        factor = NS_A * identity + NS_B * current + NS_C * square
        ortho = jnp.dot(ortho, factor, precision=PRECISE)
        if iteration + 1 < NS_ITERS:
            current = jnp.dot(
                current, jnp.dot(factor, factor, precision=PRECISE), precision=PRECISE
            )
    return -LEARN_RATE * 0.2 * math.sqrt(max(total_rows, D)) * ortho


def self_gram(matrix):
    return lax.dot_general(matrix, matrix, (((0,), (0,)), ((), ())), precision=PRECISE)


def shards(
    tokens,
    cotangent,
    segments,
    weight_in,
    weight_out,
    weight_up,
    weight_down,
    vectors,
    momentum_in,
    momentum_out,
    momentum_up,
    momentum_down,
    first_moment,
    second_moment,
):
    projection, conv_taps, gain_one, gain_two, gain_head, decay_log, decay_bias = unpack_vectors(
        vectors
    )
    full_in, full_out, full_up, full_down = (
        lax.all_gather(weight_in.astype(jnp.bfloat16), "fsdp", axis=0, tiled=True),
        lax.all_gather(weight_out.astype(jnp.bfloat16), "fsdp", axis=0, tiled=True),
        lax.all_gather(weight_up.astype(jnp.bfloat16), "fsdp", axis=0, tiled=True),
        lax.all_gather(weight_down.astype(jnp.bfloat16), "fsdp", axis=0, tiled=True),
    )
    token_rows = tokens[0].astype(jnp.float32)
    count_rows = token_rows.shape[0]
    conv_width = 2 * H * DKH + H * DVH
    id_plus = segments[0].astype(jnp.float32) + 1.0
    normed, norm_back = jax.vjp(rms_scale, token_rows, gain_one)
    normed_low = normed.astype(jnp.bfloat16)
    projected = contract_last(normed_low, full_in).astype(jnp.bfloat16)
    conv_low = projected[:, :conv_width]
    gate_low = projected[:, conv_width:]
    edge_rows, edge_ids = passed_along(
        (
            conv_low[count_rows - KCONV + 1 :],
            id_plus[count_rows - KCONV + 1 :].astype(jnp.bfloat16),
        ),
        "seq",
        1,
    )
    extended_ids = jnp.concatenate([edge_ids.astype(jnp.float32), id_plus])
    extended = jnp.concatenate([edge_rows, conv_low], axis=0).astype(jnp.float32)
    identity = jnp.broadcast_to(jnp.eye(DKH, dtype=jnp.float32), (H, DKH, DKH))
    zero_state = jnp.zeros((H, DKH, DVH), jnp.float32)
    start_state = jnp.concatenate([zero_state, identity], axis=2)

    def mixer_local(conv_values, normed_values, tap_weights, small_weights, rates, rate_bias):
        return mixer_core(
            conv_values,
            extended_ids,
            normed_values,
            tap_weights,
            small_weights,
            rates,
            rate_bias,
            start_state,
            extended_ids[KCONV - 2],
        )

    (local_out, final_state), mixer_back = jax.vjp(
        mixer_local,
        extended,
        normed_low.astype(jnp.float32),
        conv_taps,
        projection,
        decay_log,
        decay_bias,
    )
    own_part = local_out[:, :, :DVH]
    reach_rows = local_out[:, :, DVH:]
    carry_state = final_state[:, :, :DVH]
    transfer = final_state[:, :, DVH:]
    prefix = entering((transfer, carry_state), "seq", compose_maps, (identity, zero_state))
    state_in = prefix[1]
    recurrent = own_part + jnp.einsum("thi,hiw->thw", reach_rows, state_in, precision=PRECISE)

    def gate_local(recurrent_values, gate_values, head_gain):
        return rms_scale(recurrent_values, head_gain).reshape(count_rows, H * DVH) * jax.nn.silu(
            gate_values
        )

    gated, gate_back = jax.vjp(gate_local, recurrent, gate_low.astype(jnp.float32), gain_head)
    gated_low = gated.astype(jnp.bfloat16)
    attention = jnp.dot(gated_low, full_out, preferred_element_type=jnp.float32)
    residual = token_rows + attention
    normed_two, norm_two_back = jax.vjp(rms_scale, residual, gain_two)
    normed_two_low = normed_two.astype(jnp.bfloat16)
    gate_up = contract_last(normed_two_low, full_up)
    hidden, swiglu_back = jax.vjp(swiglu, gate_up)
    hidden_low = hidden.astype(jnp.bfloat16)
    feed_out = jnp.dot(hidden_low, full_down, preferred_element_type=jnp.float32)
    mixed = (residual + feed_out).astype(jnp.bfloat16)[None]
    back_in, back_out, back_up, back_down = (full_in, full_out, full_up, full_down)
    grad_rows = cotangent[0].astype(jnp.float32)
    grad_feed_low = cotangent[0]
    grad_down = contract_first(hidden_low, grad_feed_low)
    grad_hidden = contract_last(grad_feed_low, back_down)
    (grad_gate_up,) = swiglu_back(grad_hidden)
    grad_gate_up_low = grad_gate_up.astype(jnp.bfloat16)
    grad_up = contract_first(grad_gate_up_low, normed_two_low)
    grad_normed_two = jnp.dot(grad_gate_up_low, back_up, preferred_element_type=jnp.float32)
    grad_resid_part, grad_gain_two = norm_two_back(grad_normed_two)
    grad_residual = grad_rows + grad_resid_part
    grad_attn_low = grad_residual.astype(jnp.bfloat16)
    grad_wout = contract_first(gated_low, grad_attn_low)
    grad_gated = contract_last(grad_attn_low, back_out)
    grad_recurrent, grad_gate_in, grad_gain_head = gate_back(grad_gated)
    grad_state_local = jnp.einsum("thi,thw->hiw", reach_rows, grad_recurrent, precision=PRECISE)
    grad_reach = jnp.einsum("thw,hiw->thi", grad_recurrent, state_in, precision=PRECISE)
    back_prefix = prefix_2(
        (jnp.swapaxes(transfer, 1, 2), grad_state_local),
        "seq",
        compose_maps,
        (identity, zero_state),
    )
    grad_after = back_prefix[1]
    grad_transfer = jnp.einsum("hiw,hjw->hij", grad_after, state_in, precision=PRECISE)
    grad_outputs = jnp.concatenate([grad_recurrent, grad_reach], axis=2)
    grad_final = jnp.concatenate([grad_after, grad_transfer], axis=2)
    (
        grad_extended,
        grad_normed_small,
        grad_taps,
        grad_projection,
        grad_decay_log,
        grad_decay_bias,
    ) = mixer_back((grad_outputs, grad_final))
    from_next = passed_along(grad_extended[: KCONV - 1].astype(jnp.bfloat16), "seq", -1).astype(
        jnp.float32
    )
    grad_conv = grad_extended[KCONV - 1 :]
    grad_conv = jnp.concatenate(
        [grad_conv[: count_rows - KCONV + 1], grad_conv[count_rows - KCONV + 1 :] + from_next],
        axis=0,
    )
    grad_projected_low = jnp.concatenate([grad_conv, grad_gate_in], axis=1).astype(jnp.bfloat16)
    grad_win = contract_first(grad_projected_low, normed_low)
    grad_normed = (
        jnp.dot(grad_projected_low, back_in, preferred_element_type=jnp.float32) + grad_normed_small
    )
    grad_token_part, grad_gain_one = norm_back(grad_normed)
    grad_tokens = (grad_residual + grad_token_part)[None]
    reduced_in, reduced_out, reduced_up, reduced_down = (
        lax.psum_scatter(grad_win, ("seq", "fsdp"), scatter_dimension=0, tiled=True),
        lax.psum_scatter(grad_wout, ("seq", "fsdp"), scatter_dimension=0, tiled=True),
        lax.psum_scatter(grad_up, ("seq", "fsdp"), scatter_dimension=0, tiled=True),
        lax.psum_scatter(grad_down, ("seq", "fsdp"), scatter_dimension=0, tiled=True),
    )
    grad_vector_part = jnp.concatenate(
        [
            grad_projection.reshape(-1),
            grad_taps.reshape(-1),
            grad_gain_one,
            grad_gain_two,
            grad_gain_head,
            grad_decay_log,
            grad_decay_bias,
        ]
    )
    squares_local = (
        jnp.sum(reduced_in * reduced_in)
        + jnp.sum(reduced_out * reduced_out)
        + jnp.sum(reduced_up * reduced_up)
        + jnp.sum(reduced_down * reduced_down)
    )
    grad_vector, squares_total = lax.psum((grad_vector_part, squares_local), ("seq", "fsdp"))
    grad_norm = jnp.sqrt(squares_total + jnp.sum(grad_vector * grad_vector))
    clipping = jnp.minimum(1.0, CLIP_NORM / (grad_norm + 1e-06))
    renewed_in = MOMENTUM * momentum_in + (1.0 - MOMENTUM) * clipping * reduced_in
    renewed_out = MOMENTUM * momentum_out + (1.0 - MOMENTUM) * clipping * reduced_out
    renewed_up = MOMENTUM * momentum_up + (1.0 - MOMENTUM) * clipping * reduced_up
    renewed_down = MOMENTUM * momentum_down + (1.0 - MOMENTUM) * clipping * reduced_down
    gram_in, gram_out, gram_up, gram_down = lax.psum(
        (
            self_gram(renewed_in),
            self_gram(renewed_out),
            self_gram(renewed_up),
            self_gram(renewed_down),
        ),
        ("seq", "fsdp"),
    )
    devices_all = lax.axis_size(("seq", "fsdp"))
    update_in = muon_update(renewed_in, gram_in, renewed_in.shape[0] * devices_all)
    update_out = muon_update(renewed_out, gram_out, renewed_out.shape[0] * devices_all)
    update_up = muon_update(renewed_up, gram_up, renewed_up.shape[0] * devices_all)
    update_down = muon_update(renewed_down, gram_down, renewed_down.shape[0] * devices_all)
    clipped = clipping * grad_vector
    first_next = ADAM_ONE * first_moment + (1.0 - ADAM_ONE) * clipped
    second_next = ADAM_TWO * second_moment + (1.0 - ADAM_TWO) * clipped * clipped
    update_vector = (
        -VECTOR_RATE
        * (first_next / (1.0 - ADAM_ONE**STEP))
        / (jnp.sqrt(second_next / (1.0 - ADAM_TWO**STEP)) + ADAM_EPS)
    )
    return (
        mixed,
        grad_tokens,
        reduced_in,
        reduced_out,
        reduced_up,
        reduced_down,
        renewed_in,
        renewed_out,
        renewed_up,
        renewed_down,
        update_in,
        update_out,
        update_up,
        update_down,
        grad_vector,
        first_next,
        second_next,
        update_vector,
        grad_norm.reshape(1),
    )


Z_LINE = ("seq", (1, 2))
X_PAIR = ("seq", (0,))
Y_PAIR = ("fsdp", (1,))
CORES = ("fsdp", (0,))
SEQ_LAYOUT = (Z_LINE, X_PAIR)
FSDP_LAYOUT = (Y_PAIR, CORES)


def exchanged(value, group, offset):
    axis, bits = group
    mask = sum(1 << bit for i, bit in enumerate(bits) if (offset >> i) & 1)
    return lax.ppermute(value, axis, [(i, i ^ mask) for i in range(lax.axis_size(axis))])


def place_in(group):
    axis, bits = group
    mine = lax.axis_index(axis)
    return sum(((mine >> bit) & 1) << i for i, bit in enumerate(bits))


def picked(value, index, position=0):
    return lax.dynamic_index_in_dim(value, index, position, keepdims=False)


def scattered_sum(parts, layout, order, wire=jnp.bfloat16, lead=0):
    sizes = tuple(2 ** len(bits) for _, bits in layout)
    held = parts.reshape(parts.shape[:lead] + sizes + parts.shape[lead + 1 :])
    left = list(layout)
    for group in order:
        position, place = (lead + left.index(group), place_in(group))
        total = picked(held, place, position).astype(jnp.float32)
        for offset in range(1, 2 ** len(group[1])):
            gone = picked(held, place ^ offset, position).astype(wire)
            total = total + exchanged(gone, group, offset).astype(jnp.float32)
        held = total
        left.remove(group)
    return held


def gathered(value, layout, order):
    held = value
    done = []
    for group in order:
        count, place = (2 ** len(group[1]), place_in(group))
        pieces = [held] + [exchanged(held, group, offset) for offset in range(1, count)]
        rows = []
        for k in range(count):
            row = pieces[0]
            for offset in range(1, count):
                row = jnp.where((place ^ k) == offset, pieces[offset], row)
            rows.append(row)
        spot = sum(1 for other in done if layout.index(other) < layout.index(group))
        held = jnp.stack(rows, axis=spot)
        done.append(group)
    return held.reshape((-1,) + value.shape)


def summed_over(value, group_list):
    for group in group_list:
        others = [exchanged(value, group, offset) for offset in range(1, 2 ** len(group[1]))]
        value = sum(others, value)
    return value


def matchings(targets, slots, count):
    remaining = {src: [(dst, i) for i, (dst, _) in enumerate(targets[src])] for src in range(count)}
    rounds = []
    for _ in range(slots):
        owner = {}

        def seek(src, seen):
            for dst, i in remaining[src]:
                if dst in seen:
                    continue
                seen.add(dst)
                if dst not in owner or seek(owner[dst][0], seen):
                    owner[dst] = (src, i)
                    return True
            return False

        for src in range(count):
            assert seek(src, set())
        chosen = {}
        for dst, (src, i) in owner.items():
            chosen[src] = (dst, i)
        for src, (dst, i) in chosen.items():
            remaining[src].remove((dst, i))
        rounds.append(chosen)
    return rounds


def looked_up(entries, index):
    found = jnp.uint32(0)
    for bit in range(max(max(entries), 1).bit_length()):
        word = sum(((entry >> bit) & 1) << i for i, entry in enumerate(entries))
        one = lax.shift_right_logical(jnp.uint32(word), index.astype(jnp.uint32)) & jnp.uint32(1)
        found = found | lax.shift_left(one, jnp.uint32(bit))
    return found.astype(jnp.int32)


def routed(granules, targets, axes, me):
    slots, count = (len(targets[0]), len(targets))
    pieces = []
    for chosen in matchings(targets, slots, count):
        sent = [chosen[src][1] for src in range(count)]
        landing = [0] * count
        for src, (dst, i) in chosen.items():
            landing[dst] = targets[src][i][1]
        piece = lax.ppermute(
            picked(granules, looked_up(sent, me)), axes, [(src, chosen[src][0]) for src in range(count)]
        )
        pieces.append((piece, looked_up(landing, me)))
    return [
        sum(
            jnp.where(place == slot, piece.astype(jnp.float32), 0.0)
            for piece, place in pieces
        )
        for slot in range(slots)
    ]


CHUNK = 128
MIX = lax.Precision.HIGH


def product(spec, left, right):
    return jnp.einsum(spec, left, right, precision=MIX, preferred_element_type=jnp.float32)


def unit_inverse(strict):
    size = strict.shape[-1]
    rows = lax.broadcasted_iota(jnp.int32, (size, size), 0)
    cols = lax.broadcasted_iota(jnp.int32, (size, size), 1)
    exact = lambda a, b: jnp.einsum("nij,njk->nik", a, b, precision=PRECISE)
    eye = (rows == cols).astype(jnp.float32)[None]
    base = -jnp.where(((rows ^ cols) < 8)[None], strict, 0.0)
    second = exact(base, base)
    fourth = exact(second, second)
    inverse = eye + base
    inverse = inverse + exact(inverse, second)
    inverse = inverse + exact(inverse, fourth)
    width = 8
    while width < size:
        joint = ((rows ^ cols) < 2 * width) & ((rows ^ cols) >= width)
        inverse = inverse - exact(exact(inverse, jnp.where(joint[None], strict, 0.0)), inverse)
        width *= 2
    return inverse


@jax.custom_vjp
def solved_with(strict, right):
    return product("nij,njw->niw", unit_inverse(strict), right)


def solved_keep(strict, right):
    inverse = unit_inverse(strict)
    answer = product("nij,njw->niw", inverse, right)
    return answer, (inverse, answer)


def solved_back(kept, grad):
    inverse, answer = kept
    grad_right = product("nji,njw->niw", inverse, grad)
    return -product("niw,njw->nij", grad_right, answer), grad_right


solved_with.defvjp(solved_keep, solved_back)


def chunk_maps(queries, keys, values, beta, cumulative, linked, below, first_open):
    spread = cumulative[:, :, None] - cumulative[:, None, :]
    ratios = jnp.where(linked, jnp.exp(jnp.where(linked, spread, 0.0)), 0.0)
    carried = jnp.exp(cumulative) * first_open
    key_gram = product("ntd,nsd->nts", keys, keys)
    cross = ratios * product("ntd,nsd->nts", queries, keys)
    strict = beta[:, :, None] * jnp.where(below, ratios * key_gram, 0.0)
    right = beta[:, :, None] * jnp.concatenate([carried[:, :, None] * keys, values], axis=2)
    both = solved_with(strict, right)
    weighted = keys * ratios[:, -1, :, None]
    onward = product("nsd,nsw->ndw", weighted, both)
    outward = product("nts,nsw->ntw", cross, both)
    size = keys.shape[2]
    eye = jnp.eye(size, dtype=jnp.float32)[None]
    state_map = carried[:, -1][:, None, None] * eye - onward[:, :, :size]
    reach = carried[:, :, None] * queries - outward[:, :, :size]
    return state_map, onward[:, :, size:], reach, outward[:, :, size:]


def pair_inputs(conv_in, small, ids, taps, rate, bias):
    count = conv_in.shape[0]
    extended = jnp.concatenate([jnp.zeros((KCONV - 1, conv_in.shape[1]), jnp.float32), conv_in])
    extended_ids = jnp.concatenate([jnp.zeros((KCONV - 1,), jnp.float32), ids])
    conv_out = short_conv(extended, extended_ids, taps)
    beta = jax.nn.sigmoid(small[:, 0])
    log_decay = -jnp.exp(rate) * jax.nn.softplus(small[:, 1] + bias)
    queries = conv_out[:, :DKH]
    queries = (
        queries
        * lax.rsqrt(jnp.sum(queries * queries, axis=-1, keepdims=True) + RMS_EPS)
        * DKH ** (-0.5)
    )
    keys = conv_out[:, DKH : 2 * DKH]
    keys = keys * lax.rsqrt(jnp.sum(keys * keys, axis=-1, keepdims=True) + RMS_EPS)
    chunks = count // CHUNK
    cut = lambda a: a.reshape((chunks, CHUNK) + a.shape[1:])
    cumulative = jnp.cumsum(cut(log_decay), axis=1)
    return cut(queries), cut(keys), cut(conv_out[:, 2 * DKH :]), cut(beta), cumulative


def pair_masks(ids):
    chunks = ids.shape[0] // CHUNK
    cut = ids.reshape(chunks, CHUNK)
    rows = lax.broadcasted_iota(jnp.int32, (CHUNK, CHUNK), 0)
    cols = lax.broadcasted_iota(jnp.int32, (CHUNK, CHUNK), 1)
    linked = (rows >= cols)[None] & (cut[:, :, None] == cut[:, None, :])
    before = jnp.concatenate([jnp.zeros((1,), ids.dtype), cut[:-1, -1]])
    return linked, (rows > cols)[None], (cut == before[:, None]).astype(jnp.float32)


def states_forward(state_map, addend):
    state = jnp.zeros(addend.shape[1:], jnp.float32)
    entering_states = []
    for n in range(addend.shape[0]):
        entering_states.append(state)
        state = jnp.dot(state_map[n], state, precision=MIX) + addend[n]
    return jnp.stack(entering_states)


def states_backward(state_map, grad_entering):
    grad = jnp.zeros(grad_entering.shape[1:], jnp.float32)
    after = []
    for n in reversed(range(grad_entering.shape[0])):
        after.append(grad)
        grad = grad_entering[n] + jnp.einsum("ij,iw->jw", state_map[n], grad, precision=MIX)
    return jnp.stack(after[::-1])


BLOCK = 128
SIDE = D // BLOCK
PACK = SIDE * (SIDE + 1) // 2


def gram_kernel(clip_ref, *refs):
    count, total = (0, (len(refs) - 1) // 3)
    for one in range(total):
        momentum, grad, renewed = (refs[2 * one], refs[2 * one + 1], refs[2 * total + one])
        rows = MOMENTUM * momentum[...] + (1.0 - MOMENTUM) * clip_ref[0] * grad[...]
        renewed[...] = rows
        narrow = rows.astype(jnp.bfloat16)
        for i in range(SIDE):
            left = narrow[:, i * BLOCK : (i + 1) * BLOCK]
            panel = contract_first(left, narrow[:, i * BLOCK :])
            for j in range(SIDE - i):
                refs[-1][count] = panel[:, j * BLOCK : (j + 1) * BLOCK].astype(jnp.bfloat16)
                count += 1


def gram_blocks(clipping, momenta, grads):
    whole = pl.BlockSpec(memory_space=pltpu.VMEM)
    return pl.pallas_call(
        gram_kernel,
        in_specs=[pl.BlockSpec(memory_space=pltpu.SMEM)] + [whole] * (2 * len(grads)),
        out_specs=[whole] * (len(grads) + 1),
        out_shape=[jax.ShapeDtypeStruct(grad.shape, jnp.float32) for grad in grads]
        + [jax.ShapeDtypeStruct((len(grads) * PACK, BLOCK, BLOCK), jnp.bfloat16)],
        name="gram_blocks",
    )(clipping.reshape(1), *[array for pair in zip(momenta, grads) for array in pair])


def muon_kernel(rates, blocks_ref, *refs):
    gram_ref = refs[-1]
    line = lax.broadcasted_iota(jnp.int32, (BLOCK, BLOCK), 0)
    column = lax.broadcasted_iota(jnp.int32, (BLOCK, BLOCK), 1)
    count = 0
    for one, rate in enumerate(rates):
        rows_ref, out_ref = (refs[one], refs[len(rates) + one])
        trace = jnp.zeros((BLOCK, BLOCK), jnp.float32)
        for i in range(SIDE):
            for j in range(i, SIDE):
                block = blocks_ref[count]
                gram_ref[i * BLOCK : (i + 1) * BLOCK, j * BLOCK : (j + 1) * BLOCK] = block
                if i == j:
                    trace = trace + jnp.where(line == column, block.astype(jnp.float32), 0.0)
                else:
                    turned = block.astype(jnp.float32).T.astype(jnp.bfloat16)
                    gram_ref[j * BLOCK : (j + 1) * BLOCK, i * BLOCK : (i + 1) * BLOCK] = turned
                count += 1
        total = jnp.sum(jnp.sum(trace, axis=1, keepdims=True), axis=0, keepdims=True)
        inverse_norm = 1.0 / (jnp.sqrt(total) + 1e-07)
        squared = inverse_norm * inverse_norm

        def times(rows):
            narrow = rows.astype(jnp.bfloat16)
            return jnp.dot(narrow, gram_ref[...], preferred_element_type=jnp.float32) * squared

        def through(rows):
            once = times(rows)
            return NS_A * rows + NS_B * once + NS_C * times(once)

        def advanced(rows):
            return through(through(times(rows)))

        first = through(rows_ref[...] * inverse_norm)
        once = advanced(first)
        out_ref[...] = rate * (NS_A * first + NS_B * once + NS_C * advanced(once))


def muon_rows(rows, blocks, rates):
    whole = pl.BlockSpec(memory_space=pltpu.VMEM)
    return pl.pallas_call(
        partial(muon_kernel, rates),
        in_specs=[whole] * (1 + len(rows)),
        out_specs=[whole] * len(rows),
        out_shape=[jax.ShapeDtypeStruct(one.shape, jnp.float32) for one in rows],
        scratch_shapes=[pltpu.VMEM((D, D), jnp.bfloat16)],
        name="muon_rows",
    )(blocks, *rows)


def blocks_everywhere(blocks, order):
    own = scattered_sum(blocks.reshape(32, -1, BLOCK), order, order).astype(jnp.bfloat16)
    return gathered(own, order, order[::-1]).reshape(blocks.shape)


def head_tables(fsdp):
    per = (2 * H * DKH + 2 * H * DVH) // fsdp // DKH
    give, find = ([], [])
    for head in range(H):
        wanted = [head, H + head] + [
            2 * H + base + 2 * head + k for base in (0, 2 * H) for k in range(2)
        ]
        lists = [[g % per for g in wanted if g // per == f] for f in range(fsdp)]
        seen = [0] * fsdp
        where = []
        for g in wanted:
            f = g // per
            where.append((f, seen[f]))
            seen[f] += 1
        most = 2
        assert max(len(one) for one in lists) <= most
        give.append([one + [0] * (most - len(one)) for one in lists])
        find.append([f * most + j for f, j in where])
    return give, find


def in_targets(seq, fsdp):
    granule = 64
    per = (2 * H * DKH + 2 * H * DVH) // (seq * fsdp) // granule
    targets = []
    for s in range(seq):
        rows = []
        for start, size in (
            (s * DKH, DKH),
            (H * DKH + s * DKH, DKH),
            (2 * H * DKH + s * DVH, DVH),
            (2 * H * DKH + H * DVH + s * DVH, DVH),
        ):
            rows += [start // granule + k for k in range(size // granule)]
        for f in range(fsdp):
            own = rows[f * per : (f + 1) * per]
            targets.append([(g // per, g % per) for g in own])
    return targets


def up_targets(seq, fsdp):
    piece = FF // (seq * fsdp)
    return [
        [((f * seq + s) // 2, (f * seq + s) % 2), (seq * fsdp // 2 + (f * seq + s) // 2, (f * seq + s) % 2)]
        for s in range(seq)
        for f in range(fsdp)
    ]


def block_targets(seq, fsdp):
    return [[(f * seq + s, 0)] for s in range(seq) for f in range(fsdp)]


def up_shuffle_targets(fsdp):
    half = fsdp // 2
    return [[(2 * (f % half) + k, f // half) for k in range(2)] for f in range(fsdp)]


def pair_shards(
    tokens,
    cotangent,
    segments,
    weight_in,
    weight_out,
    weight_up,
    weight_down,
    vectors,
    momentum_in,
    momentum_out,
    momentum_up,
    momentum_down,
    first_moment,
    second_moment,
):
    seq, fsdp = (lax.axis_size("seq"), lax.axis_size("fsdp"))
    head, group = (lax.axis_index("seq"), lax.axis_index("fsdp"))
    me = head * fsdp + group
    inward, outward = ((CORES, Y_PAIR), (Y_PAIR, CORES))
    projection, conv_taps, gain_one, gain_two, gain_head, decay_log, decay_bias = unpack_vectors(
        vectors
    )
    own = tokens.shape[1]
    length = own * seq
    heads_low = jnp.bfloat16

    row_ids = jnp.zeros((16, D), heads_low)
    row_ids = row_ids.at[0, :own].set((segments[0] + 1).astype(heads_low))
    packed = lax.all_gather(jnp.concatenate([tokens[0], row_ids]), "seq")

    give, find = head_tables(fsdp)
    slices = [
        lax.dynamic_slice_in_dim(
            weight_in, looked_up([one[j] for row in give for one in row], me) * DKH, DKH, 0
        )
        for j in range(2)
    ]
    given = gathered(jnp.stack(slices).astype(heads_low), FSDP_LAYOUT, outward)
    given = given.reshape(2 * fsdp, DKH, D)
    small_rows = jnp.stack([picked(projection, head), picked(projection, H + head)])
    taps_rows = conv_taps.reshape(KCONV, 4 * H, DKH)
    taps_head = jnp.concatenate(
        [
            picked(taps_rows, head, 1),
            picked(taps_rows, H + head, 1),
            picked(taps_rows, 2 * H + 2 * head, 1),
            picked(taps_rows, 2 * H + 2 * head + 1, 1),
        ],
        axis=1,
    )
    this = lax.broadcasted_iota(jnp.int32, (H,), 0) == head
    rate, bias = [jnp.sum(jnp.where(this, one, 0.0)) for one in (decay_log, decay_bias)]

    full_out = lax.all_gather(weight_out.astype(heads_low), "fsdp", axis=0, tiled=True)
    cot_group = gathered(cotangent[0], FSDP_LAYOUT, outward).reshape(fsdp * own, D)
    half_up = weight_up.shape[0] // 2
    up_halves, given = lax.optimization_barrier(
        (weight_up.astype(heads_low).reshape(2, half_up, D), given)
    )
    up_gate, up_value = [
        part.astype(heads_low)
        for part in routed(up_halves, up_shuffle_targets(fsdp), "fsdp", group)
    ]
    token_seq = packed[:, :own].reshape(length, D)
    ids = packed[:, own, :own].reshape(length).astype(jnp.float32)
    head_rows = jnp.concatenate([picked(given, looked_up([row[j] for row in find], head)) for j in range(6)])
    low_down = weight_down.astype(heads_low)

    token_rows = token_seq.astype(jnp.float32)
    scaled_rows = token_rows * lax.rsqrt(
        jnp.mean(token_rows * token_rows, axis=-1, keepdims=True) + RMS_EPS
    )
    normed_low = (scaled_rows * gain_one).astype(heads_low)
    projected = contract_last(normed_low, head_rows).astype(heads_low)
    conv_in = projected[:, : 2 * DKH + DVH].astype(jnp.float32)
    gate_in = projected[:, 2 * DKH + DVH :].astype(jnp.float32)
    small = lax.dot_general(
        normed_low.astype(jnp.float32), small_rows, (((1,), (1,)), ((), ())), precision=PRECISE
    )
    linked, below, first_open = pair_masks(ids)
    parts, inputs_back = jax.vjp(
        lambda c, m, t, r, b: pair_inputs(c, m, ids, t, r, b),
        conv_in,
        small,
        taps_head,
        rate,
        bias,
    )
    maps, maps_back = jax.vjp(
        lambda q, k, v, b, c: chunk_maps(q, k, v, b, c, linked, below, first_open), *parts
    )
    state_map, addend, reach, local = maps
    states = states_forward(state_map, addend)
    recurrent = (product("ntd,ndw->ntw", reach, states) + local).reshape(length, DVH)

    def gate_pair(recurrent_values, gate_values, head_gain):
        return rms_scale(recurrent_values, head_gain) * jax.nn.silu(gate_values)

    gated, gate_back = jax.vjp(gate_pair, recurrent, gate_in, gain_head)
    gated_low, cot_group, up_gate, up_value = lax.optimization_barrier(
        (gated.astype(heads_low), cot_group, up_gate, up_value)
    )
    low_up = jnp.concatenate([up_gate, up_value])
    gated_own = lax.all_to_all(gated_low.reshape(seq, own, DVH), "seq", 0, 0)
    gated_own = jnp.transpose(gated_own, (1, 0, 2)).reshape(own, H * DVH)

    own_rows = tokens[0].astype(jnp.float32)
    residual = own_rows + jnp.dot(gated_own, full_out, preferred_element_type=jnp.float32)
    normed_two, norm_two_back = jax.vjp(rms_scale, residual, gain_two)
    two_group = gathered(normed_two.astype(heads_low), FSDP_LAYOUT, outward)
    two_group = two_group.reshape(fsdp * own, D)
    gate_up = contract_last(two_group, low_up)
    units = half_up

    def swiglu_own(values):
        return jax.nn.silu(values[:, :units]) * values[:, units:]

    hidden, swiglu_back = jax.vjp(swiglu_own, gate_up)
    hidden_low = hidden.astype(heads_low)
    feed_parts = jnp.dot(hidden_low, low_down, preferred_element_type=jnp.float32)
    feed_out = scattered_sum(feed_parts.reshape(fsdp, own, D), FSDP_LAYOUT, inward)
    mixed = (residual + feed_out).astype(heads_low)[None]

    grad_hidden = contract_last(cot_group, low_down)
    (grad_gate_up,) = swiglu_back(grad_hidden)
    grad_gate_up_low = grad_gate_up.astype(heads_low)
    two_parts = jnp.dot(grad_gate_up_low, low_up, preferred_element_type=jnp.float32)

    over_seq = lambda parts, lead=0: scattered_sum(
        parts, SEQ_LAYOUT, (X_PAIR, Z_LINE), lead=lead
    ).astype(heads_low)
    piece = FF // (seq * fsdp)
    grad_up_part = contract_first(grad_gate_up_low, two_group).astype(heads_low)
    up_own = over_seq(grad_up_part.reshape(2, seq, piece, D), 1)
    grad_down_part = contract_first(hidden_low, cot_group).astype(heads_low)
    down_own = over_seq(grad_down_part.reshape(seq, piece, D))
    grad_normed_two = scattered_sum(two_parts.reshape(fsdp, own, D), FSDP_LAYOUT, inward)
    grad_resid_part, grad_gain_two = norm_two_back(grad_normed_two)
    grad_residual = cotangent[0].astype(jnp.float32) + grad_resid_part
    grad_attn_low = grad_residual.astype(heads_low)
    grad_gated_own = contract_last(grad_attn_low, full_out).astype(heads_low)
    grad_gated_own = jnp.transpose(grad_gated_own.reshape(own, seq, DVH), (1, 0, 2))
    grad_gated = lax.all_to_all(grad_gated_own, "seq", 0, 0).reshape(length, DVH)

    gated_group = lax.all_to_all(gated_own.reshape(own, fsdp, -1), "fsdp", 1, 0)
    attn_group = gathered(grad_attn_low, FSDP_LAYOUT, outward).reshape(fsdp * own, D)
    grad_out_part = contract_first(gated_group.reshape(fsdp * own, -1), attn_group)
    out_own = over_seq(grad_out_part.astype(heads_low).reshape(seq, -1, D))
    both = ("seq", "fsdp")
    (reduced_block,) = routed(
        jnp.concatenate([down_own, out_own])[None], block_targets(seq, fsdp), both, me
    )
    reduced_down, reduced_out = (reduced_block[:piece], reduced_block[piece:])
    reduced_up = jnp.concatenate(routed(up_own, up_targets(seq, fsdp), both, me))

    grad_gated = grad_gated.astype(jnp.float32)
    grad_recurrent, grad_gate_in, grad_gain_head = gate_back(grad_gated)
    grad_out_chunks = grad_recurrent.reshape(local.shape)
    grad_entering = product("ntd,ntw->ndw", reach, grad_out_chunks)
    grad_after = states_backward(state_map, grad_entering)
    grad_maps = (
        product("niw,njw->nij", grad_after, states),
        grad_after,
        product("ntw,ndw->ntd", grad_out_chunks, states),
        grad_out_chunks,
    )
    grad_conv, grad_small, grad_taps, grad_rate, grad_bias = inputs_back(maps_back(grad_maps))
    grad_projected_low = jnp.concatenate([grad_conv, grad_gate_in], axis=1).astype(heads_low)
    grad_in_part = contract_first(grad_projected_low, normed_low)
    normed_parts = jnp.dot(grad_projected_low, head_rows, preferred_element_type=jnp.float32)
    normed_parts = normed_parts + jnp.dot(grad_small, small_rows, precision=PRECISE)
    normed_low_parts = normed_parts.astype(heads_low).reshape(seq, own, D)
    normed_left = scattered_sum(normed_low_parts[..., : D // 2], SEQ_LAYOUT, (X_PAIR, Z_LINE))
    normed_right = scattered_sum(normed_low_parts[..., D // 2 :], SEQ_LAYOUT, (X_PAIR, Z_LINE))
    grad_normed = jnp.concatenate([normed_left, normed_right], axis=-1)
    _, norm_back = jax.vjp(rms_scale, own_rows, gain_one)
    grad_token_part, _ = norm_back(grad_normed)
    grad_gain_one = jnp.sum(normed_parts * scaled_rows, axis=0)
    grad_tokens = (grad_residual + grad_token_part)[None]
    in_rows = grad_in_part.shape[0] // fsdp
    in_own = scattered_sum(grad_in_part.reshape(fsdp, in_rows, D), FSDP_LAYOUT, inward)
    in_own = in_own.astype(heads_low)
    in_granules = in_own.reshape(in_rows // 64, 64, D)
    reduced_in = jnp.concatenate(routed(in_granules, in_targets(seq, fsdp), both, me))

    grad_projection = lax.dot_general(
        grad_small, normed_low.astype(jnp.float32), (((0,), (0,)), ((), ())), precision=PRECISE
    )
    width = 2 * DKH + DVH
    square = lambda part: jnp.sum(jnp.square(part.astype(jnp.float32)))
    compact = jnp.concatenate(
        [
            grad_projection.reshape(-1),
            grad_taps.reshape(-1),
            grad_gain_one,
            grad_gain_two,
            grad_gain_head,
            grad_rate.reshape(1),
            grad_bias.reshape(1),
            (square(in_own) + square(up_own) + square(down_own) + square(out_own)).reshape(1),
        ]
    )
    fill = -compact.shape[0] % 1024
    compact = jnp.concatenate([compact, jnp.zeros((fill,), jnp.float32)]).reshape(-1, 128)
    compact = summed_over(compact, [("fsdp", (0, 1))])
    compact = gathered(compact, SEQ_LAYOUT, (X_PAIR, Z_LINE)).reshape(seq, -1)
    cuts = [2 * D, KCONV * width, D, D, DVH, 1, 1, 1]
    places = [sum(cuts[:i]) for i in range(len(cuts))]
    take = lambda i: compact[:, places[i] : places[i] + cuts[i]]
    taps_all = take(1).reshape(seq, KCONV, width)
    spread_taps = lambda a, b: jnp.transpose(taps_all[:, :, a:b], (1, 0, 2)).reshape(KCONV, -1)
    grad_vector = jnp.concatenate(
        [
            jnp.transpose(take(0).reshape(seq, 2, D), (1, 0, 2)).reshape(-1),
            jnp.concatenate(
                [spread_taps(0, DKH), spread_taps(DKH, 2 * DKH), spread_taps(2 * DKH, width)],
                axis=1,
            ).reshape(-1),
            jnp.sum(take(2), axis=0),
            jnp.sum(take(3), axis=0),
            jnp.sum(take(4), axis=0),
            take(5).reshape(-1),
            take(6).reshape(-1),
        ]
    )

    squares = jnp.sum(take(7))
    grad_norm = jnp.sqrt(squares + jnp.sum(grad_vector * grad_vector))
    clipping = jnp.minimum(1.0, CLIP_NORM / (grad_norm + 1e-06))
    reduced = (reduced_in, reduced_out, reduced_up, reduced_down)
    momenta = (momentum_in, momentum_out, momentum_up, momentum_down)
    renewed, updates = ([], [])
    for first, order in ((0, (CORES, Y_PAIR, X_PAIR, Z_LINE)), (2, (CORES, X_PAIR, Y_PAIR, Z_LINE))):
        *rows, blocks = gram_blocks(
            clipping, momenta[first : first + 2], reduced[first : first + 2]
        )
        rates = [
            -LEARN_RATE * 0.2 * math.sqrt(max(one.shape[0] * seq * fsdp, D)) for one in rows
        ]
        renewed += rows
        updates += muon_rows(rows, blocks_everywhere(blocks, order), rates)
    clipped = clipping * grad_vector
    first_next = ADAM_ONE * first_moment + (1.0 - ADAM_ONE) * clipped
    second_next = ADAM_TWO * second_moment + (1.0 - ADAM_TWO) * clipped * clipped
    update_vector = (
        -VECTOR_RATE
        * (first_next / (1.0 - ADAM_ONE**STEP))
        / (jnp.sqrt(second_next / (1.0 - ADAM_TWO**STEP)) + ADAM_EPS)
    )
    return (
        mixed,
        grad_tokens,
        *reduced,
        *renewed,
        *updates,
        grad_vector,
        first_next,
        second_next,
        update_vector,
        grad_norm.reshape(1),
    )


def fits_pairs(mesh, sequences):
    seq, fsdp = (mesh.shape["seq"], mesh.shape["fsdp"])
    return seq == H and fsdp == 4 and sequences == fsdp


def solution(mesh):
    in_specs = (
        P("fsdp", "seq", None),
        P("fsdp", "seq", None),
        P("fsdp", "seq"),
        P("fsdp", None),
        P("fsdp", None),
        P("fsdp", None),
        P("fsdp", None),
        P(),
        P(("seq", "fsdp"), None),
        P(("seq", "fsdp"), None),
        P(("seq", "fsdp"), None),
        P(("seq", "fsdp"), None),
        P(),
        P(),
    )
    out_specs = (
        P("fsdp", "seq", None),
        P("fsdp", "seq", None),
        P(("seq", "fsdp"), None),
        P(("seq", "fsdp"), None),
        P(("seq", "fsdp"), None),
        P(("seq", "fsdp"), None),
        P(("seq", "fsdp"), None),
        P(("seq", "fsdp"), None),
        P(("seq", "fsdp"), None),
        P(("seq", "fsdp"), None),
        P(("seq", "fsdp"), None),
        P(("seq", "fsdp"), None),
        P(("seq", "fsdp"), None),
        P(("seq", "fsdp"), None),
        P(),
        P(),
        P(),
        P(),
        P(),
    )

    def step(tokens, *rest):
        local = pair_shards if fits_pairs(mesh, tokens.shape[0]) else shards
        return jax.shard_map(
            local, mesh=mesh, in_specs=in_specs, out_specs=out_specs, check_vma=False
        )(tokens, *rest)

    return step
```
